32 devices in a mesh: pat: 4 (over x, core), slab: 8 (over z, y).
Axes of the slice: x: 2, y: 2, z: 4, core: 2. Of those that a mesh axis runs over, the one named last changes fastest.
Arguments:
- features: bfloat16 [4, 64, 48, 384], P('pat', None, 'slab'), may hold values from -50 to 50
- cotangent: bfloat16 [4, 64, 48, 384], P('pat', None, 'slab'), may hold values from -50 to 50
- weights: float32 [2, 64, 1728], replicated, may hold values from -0.15625 to 0.15625
- prev_state: float32 [2, 64, 1728], replicated, may hold values from -6 to 6
- tree_noise: float32 [2, 64, 1728], replicated, may hold values from -6 to 6
Outputs:
- state_next: float32 [2, 64, 1728], replicated
- weights_next: float32 [2, 64, 1728], replicated
The draws below stay inside these ranges and needn't reach their ends.
All inputs are finite; a program needn't handle non-finite values.
Results may differ from the reference program's by a relative error of at most 0.006.
Values may be sent and summed in bfloat16 or wider, within the bound.
No kernel may reach another device: no remote copies, remote signals or barrier semaphores. Data moves between devices by JAX's collectives and lax.ppermute only.
A program may use at most 64 MiB of HBM per device.

```python
import jax
import jax.numpy as jnp
from jax import lax

C = 64
H = 16
W = 24
PATIENTS = 4
NZ = 48


def rough_volume(key, depth_slope):
    subkeys = jax.random.split(key, 3)
    raw_values = jnp.clip(jax.random.normal(subkeys[0], (PATIENTS, C, NZ, H * W), jnp.float32), -4.0, 4.0)
    depth_frac = jnp.arange(NZ, dtype=jnp.float32) / max(NZ - 1, 1)
    cell_exp = jax.random.uniform(subkeys[1], (PATIENTS, 1, NZ, H * W), jnp.float32, 0.0, 0.5)
    chan_exp = jax.random.uniform(subkeys[2], (PATIENTS, C, 1, 1), jnp.float32, 0.0, 0.5)
    magnitude = 10.0 ** (depth_slope * depth_frac[None, None, :, None] + cell_exp + chan_exp - 0.5 * (depth_slope + 1.0))
    return raw_values * magnitude


def draw_features(key, part):
    return rough_volume(jax.random.fold_in(key, 11), 0.48).astype(jnp.bfloat16)


def draw_cotangent(key, part):
    return rough_volume(jax.random.fold_in(key, 23), 0.48).astype(jnp.bfloat16)


def centred(own_key, extent, scale, most, kind=jnp.bfloat16):
    array = jax.random.normal(own_key, extent, jnp.float32) * scale
    return jnp.minimum(jnp.maximum(array, -most), most).astype(kind)


def setup_inputs(seed: int = 0) -> dict:
    streams_of = jax.random.split(jax.random.key(seed), 6)
    features = draw_features(jax.random.fold_in(streams_of[5], 71), 0)
    cotangent = draw_cotangent(jax.random.fold_in(streams_of[5], 71), 0)
    weights = centred(streams_of[2], (2, C, 27 * C), (27 * C) ** -0.5, 0.15625, jnp.float32)
    prev_state = centred(streams_of[3], (2, C, 27 * C), 1.0, 6.0, jnp.float32)
    tree_noise = centred(streams_of[4], (2, C, 27 * C), 1.0, 6.0, jnp.float32)
    return dict(features=features, cotangent=cotangent, weights=weights, prev_state=prev_state, tree_noise=tree_noise)


eps_norm = 1e-05
clip_bound = 400.0
step_rate = 0.1

def convolve(volume, kernel):
    channels = kernel.shape[0]
    filters = kernel.reshape(channels, 3, 3, 3, channels).transpose(0, 4, 1, 2, 3)
    result = lax.conv_general_dilated(volume[None], filters, (1, 1, 1), ((1, 1), (1, 1), (1, 1)), dimension_numbers=('NCDHW', 'OIDHW', 'NCDHW'), precision=lax.Precision.HIGHEST)
    return result[0]

def normalize(summed):
    centre = lax.optimization_barrier(jnp.mean(summed, axis=(1, 2, 3), keepdims=True))
    squares = lax.optimization_barrier(jnp.mean(summed * summed, axis=(1, 2, 3), keepdims=True))
    spread = lax.rsqrt(squares - centre * centre + eps_norm)
    return ((summed - centre) * spread, spread)

def norm_back(gradient, normed, spread):
    first = lax.optimization_barrier(jnp.mean(gradient, axis=(1, 2, 3), keepdims=True))
    second = lax.optimization_barrier(jnp.mean(gradient * normed, axis=(1, 2, 3), keepdims=True))
    return spread * (gradient - first - normed * second)

def silu_slope(values):
    sigmoid_val = jax.nn.sigmoid(values)
    return sigmoid_val * (1.0 + values * (1.0 - sigmoid_val))

def to_half(values):
    rounded = lax.optimization_barrier(values.astype(jnp.bfloat16))
    return rounded.astype(jnp.float32)

def patient_grad(volume, upstream, kernel_one, kernel_two):
    channels, planes, plane_size = volume.shape
    shaped = (channels, planes, H, W)
    inputs = volume.astype(jnp.float32).reshape(shaped)
    normed_one, spread_one = normalize(convolve(inputs, kernel_one))
    hidden = to_half(jax.nn.silu(normed_one))
    normed_two, spread_two = normalize(convolve(hidden, kernel_two))
    gradient_two = upstream.astype(jnp.float32).reshape(shaped) * silu_slope(normed_two)
    cotan_two = to_half(norm_back(gradient_two, normed_two, spread_two))
    unused, pull_two = jax.vjp(convolve, hidden, kernel_two)
    back_hidden, kgrad_two = pull_two(cotan_two)
    gradient_one = back_hidden * silu_slope(normed_one)
    cotan_one = to_half(norm_back(gradient_one, normed_one, spread_one))

    def first_layer(kernel):
        return convolve(inputs, kernel)
    unused_one, pull_one = jax.vjp(first_layer, kernel_one)
    kgrad_one = pull_one(cotan_one)[0]
    return jnp.stack([kgrad_one, kgrad_two])

def reference(features, cotangent, weights, prev_state, tree_noise):
    kernels = to_half(weights)

    def accumulate(running, patient):
        gradient = patient_grad(patient[0], patient[1], kernels[0], kernels[1])
        length = jnp.sqrt(jnp.sum(gradient * gradient))
        factor = clip_bound / jnp.maximum(length, clip_bound)
        return (running + factor * gradient, None)
    combined, unused = lax.scan(accumulate, jnp.zeros(weights.shape, jnp.float32), (features, cotangent))
    state_next = prev_state + combined
    weights_next = weights - step_rate * (combined + tree_noise)
    return (state_next, weights_next)
```

```python
import functools

import jax
import jax.numpy as jnp
from jax import lax
from jax.experimental import pallas as pl
from jax.experimental.pallas import tpu as pltpu
from jax.sharding import PartitionSpec as P

W = 24

eps_norm = 1e-05
clip_bound = 400.0
step_rate = 0.1

f32 = jnp.float32
bf16 = jnp.bfloat16

AXES = ("pat", "slab")
PAD = 128
FEATURE_HALO = 3
COTAN_HALO = 1


def call(kernel, out_shape, *args, scratch=(), flops=0):
    vmem = pl.BlockSpec(memory_space=pltpu.VMEM)
    outs = out_shape if isinstance(out_shape, (tuple, list)) else (out_shape,)
    size = sum(a.size * a.dtype.itemsize for a in args)
    return pl.pallas_call(
        kernel,
        out_shape=out_shape,
        in_specs=[vmem] * len(args),
        out_specs=jax.tree.map(lambda _: vmem, out_shape),
        scratch_shapes=list(scratch),
        cost_estimate=pl.CostEstimate(flops=flops, bytes_accessed=size, transcendentals=0),
        compiler_params=pltpu.CompilerParams(vmem_limit_bytes=40 * 2**20),
    )(*args)


def sds(shape, dtype):
    return jax.ShapeDtypeStruct(shape, dtype)


def column_masks(cells):
    column = lax.broadcasted_iota(jnp.int32, (1, cells), 1) % W
    return (column != W - 1).astype(bf16), (column != 0).astype(bf16)


def patches(planes, edge, stack):
    channels, cells = planes[0].shape
    not_last, not_first = column_masks(cells)
    edge[...] = jnp.zeros_like(edge)
    for z, plane in enumerate(planes):
        edge[0:channels, PAD + 1 : PAD + 1 + cells] = plane * not_last
        edge[channels : 2 * channels, PAD : PAD + cells] = plane
        edge[2 * channels : 3 * channels, PAD - 1 : PAD - 1 + cells] = plane * not_first
        for b in range(3):
            start = PAD + (b - 1) * W
            stack[b * 3 * channels : (b + 1) * 3 * channels, z * cells : (z + 1) * cells] = edge[
                :, start : start + cells
            ]


def tap_products(kernel, stack, product, planes, cells):
    for z in range(0, planes, 2):
        span = slice(z * cells, min(z + 2, planes) * cells)
        product[:, span] = jnp.dot(kernel[...], stack[:, span], preferred_element_type=f32)


def depth_sum(product, z, channels, cells):
    return (
        product[0:channels, z * cells : (z + 1) * cells]
        + product[channels : 2 * channels, (z + 1) * cells : (z + 2) * cells]
        + product[2 * channels : 3 * channels, (z + 2) * cells : (z + 3) * cells]
    )


def eye(size):
    return lax.broadcasted_iota(jnp.int32, (size, size), 0) == lax.broadcasted_iota(
        jnp.int32, (size, size), 1
    )


def to_row(first, second):
    both = jnp.concatenate([first, second], axis=0)
    size = both.shape[0]
    return jnp.sum(jnp.where(eye(size), both, 0.0), axis=0, keepdims=True)


def to_columns(rows):
    row = jnp.sum(rows, axis=0, keepdims=True)
    size = row.shape[1]
    both = jnp.sum(jnp.where(eye(size), row, 0.0), axis=1, keepdims=True)
    return both[: size // 2], both[size // 2 :]


def moments(rows, cell_count):
    totals, squares = to_columns(rows)
    centre = totals / cell_count
    return centre, lax.rsqrt(squares / cell_count - centre * centre + eps_norm)


def sigmoid(values):
    return 1.0 / (1.0 + jnp.exp(-values))


def slope(values):
    gate = sigmoid(values)
    return gate * (1.0 + values * (1.0 - gate))


def add_to(total, value):
    return value if total is None else total + value


def send_totals(ref, first, second):
    row = to_row(
        jnp.sum(first, axis=1, keepdims=True), jnp.sum(second, axis=1, keepdims=True)
    )
    ref[...] = jnp.broadcast_to(row, ref.shape)


def inside(z, halo, depth, slab, peers, value):
    if z < halo:
        return jnp.where(slab > 0, value, jnp.zeros_like(value))
    if z >= halo + depth:
        return jnp.where(slab < peers - 1, value, jnp.zeros_like(value))
    return value


def kernel_stacks(weights, one, two, back):
    channels = weights.shape[1]
    width = 9 * channels
    for k, target in ((0, one), (1, two)):
        rounded = weights[k].astype(bf16)
        for a in range(3):
            target[a * channels : (a + 1) * channels, :] = rounded[:, a * width : (a + 1) * width]
    turned = weights[1].T
    for a in range(3):
        for tap in range(9):
            block = (2 - a) * 9 + 8 - tap
            back[
                a * channels : (a + 1) * channels, tap * channels : (tap + 1) * channels
            ] = turned[block * channels : (block + 1) * channels, :].astype(bf16)


def field_halo(own, even_recv, odd_recv, start, count, slab, peers):
    even = slab % 2 == 0
    zero = jnp.zeros(own.shape[1:], own.dtype)
    before, after = [], []
    for z in range(start, start + count):
        x, y = even_recv[z], odd_recv[z]
        before.append(jnp.where(slab == 0, zero, jnp.where(even, y, x)))
        after.append(jnp.where(slab == peers - 1, zero, jnp.where(even, x, y)))
    return before + [own[z] for z in range(own.shape[0])] + after


def first_conv(peers, own, even_recv, odd_recv, kernel, first, totals, edge, stack, product):
    slab = lax.axis_index("slab")
    depth, channels, cells = own.shape
    planes = field_halo(own, even_recv, odd_recv, 0, FEATURE_HALO, slab, peers)
    patches(planes, edge, stack)
    tap_products(kernel, stack, product, len(planes), cells)
    s = q = None
    for z in range(depth + 4):
        value = depth_sum(product, z, channels, cells)
        first[z] = value
        if 2 <= z < depth + 2:
            s, q = add_to(s, value), add_to(q, value * value)
    send_totals(totals, s, q)


def second_conv(peers, cell_count, rows, first, kernel, hidden, second, totals, edge, stack, product):
    slab = lax.axis_index("slab")
    extended, channels, cells = first.shape
    depth = extended - 4
    centre, spread = moments(rows[...], cell_count)
    planes = []
    for z in range(extended):
        normed = (first[z] - centre) * spread
        value = inside(z, 2, depth, slab, peers, (normed * sigmoid(normed)).astype(bf16))
        planes.append(value)
        if 1 <= z < extended - 1:
            hidden[z - 1] = value
    patches(planes, edge, stack)
    tap_products(kernel, stack, product, extended, cells)
    s = q = None
    for z in range(depth + 2):
        value = depth_sum(product, z, channels, cells)
        second[z] = value
        if 1 <= z < depth + 1:
            s, q = add_to(s, value), add_to(q, value * value)
    send_totals(totals, s, q)


def second_gradient(peers, cell_count, rows, second, cotan, even_recv, odd_recv, gradient, totals):
    slab = lax.axis_index("slab")
    depth = cotan.shape[0]
    upstream = field_halo(cotan, even_recv, odd_recv, FEATURE_HALO, COTAN_HALO, slab, peers)
    centre, spread = moments(rows[...], cell_count)
    s = q = None
    for z in range(depth + 2):
        normed = (second[z] - centre) * spread
        value = upstream[z].astype(f32) * slope(normed)
        gradient[z] = value
        if 1 <= z < depth + 1:
            s, q = add_to(s, value), add_to(q, value * normed)
    send_totals(totals, s, q)


def back_conv(
    peers, cell_count, rows_one, rows_two, rows, first, second, gradient, kernel,
    cotan_two, gradient_one, totals, edge, stack, product,
):
    slab = lax.axis_index("slab")
    extended, channels, cells = second.shape
    depth = extended - 2
    centre, spread = moments(rows_two[...], cell_count)
    mean, crossed = (x / cell_count for x in to_columns(rows[...]))
    planes = []
    for z in range(extended):
        normed = (second[z] - centre) * spread
        value = (spread * (gradient[z] - mean - normed * crossed)).astype(bf16)
        value = inside(z, 1, depth, slab, peers, value)
        planes.append(value)
        if 1 <= z < depth + 1:
            cotan_two[z - 1] = value
    patches(planes, edge, stack)
    tap_products(kernel, stack, product, extended, cells)
    centre, spread = moments(rows_one[...], cell_count)
    s = q = None
    for z in range(depth):
        normed = (first[z + 2] - centre) * spread
        value = depth_sum(product, z, channels, cells) * slope(normed)
        gradient_one[z] = value
        s, q = add_to(s, value), add_to(q, value * normed)
    send_totals(totals, s, q)


def correlate(planes, cotans, edge, stack, taps):
    depth, (channels, cells) = len(cotans), cotans[0].shape
    patches(planes, edge, stack)
    zero = jnp.zeros((channels, cells), bf16)
    for a in range(3):
        for z in range(depth + 2):
            inner = 0 <= z - a < depth
            taps[a * channels : (a + 1) * channels, z * cells : (z + 1) * cells] = (
                cotans[z - a] if inner else zero
            )
    return lax.dot_general(
        stack[...], taps[...], (((1,), (1,)), ((), ())), preferred_element_type=f32
    )


def kernel_grads(
    peers, cell_count, rows_one, rows, first, gradient_one, cotan_two, hidden, own, even_recv, odd_recv,
    pieces, edge, stack, taps, gathered,
):
    slab = lax.axis_index("slab")
    depth, channels, cells = own.shape
    count, length, _ = pieces.shape
    centre, spread = moments(rows_one[...], cell_count)
    mean, crossed = (x / cell_count for x in to_columns(rows[...]))
    cotans = []
    for z in range(depth):
        normed = (first[z + 2] - centre) * spread
        cotans.append((spread * (gradient_one[z] - mean - normed * crossed)).astype(bf16))
    planes = field_halo(own, even_recv, odd_recv, 0, FEATURE_HALO, slab, peers)
    width = 9 * channels
    grads = (
        correlate(planes[FEATURE_HALO - 1 : depth + FEATURE_HALO + 1], cotans, edge, stack, taps),
        None,
    )
    for k in range(2):
        if k == 0:
            grad = grads[0]
        else:
            grad = correlate(
                [hidden[z] for z in range(depth + 2)],
                [cotan_two[z] for z in range(depth)],
                edge,
                stack,
                taps,
            )
        for a in range(3):
            gathered[a * width : (a + 1) * width, k * channels : (k + 1) * channels] = grad[
                :, a * channels : (a + 1) * channels
            ]
    if count * length > 3 * width:
        gathered[3 * width :, :] = jnp.zeros((count * length - 3 * width, 2 * channels), f32)
    for j in range(count):
        pieces[j] = gathered[j * length : (j + 1) * length, :].astype(bf16)


def piece_sums(patients, pieces, sums, squares):
    count, length, lanes = pieces.shape
    peers = count // patients
    lane = lax.broadcasted_iota(jnp.int32, (1, squares.shape[1]), 1)
    row = jnp.zeros((1, squares.shape[1]), f32)
    for p in range(patients):
        total = None
        for j in range(peers):
            total = add_to(total, pieces[p * peers + j].astype(f32))
        sums[p] = total
        part = jnp.sum(jnp.sum(total * total, axis=0, keepdims=True), axis=1, keepdims=True)
        row = jnp.where(lane == p, part, row)
    squares[...] = jnp.broadcast_to(row, squares.shape)


def clipped(patients, squares, sums, pieces):
    row = jnp.sum(squares[...], axis=0, keepdims=True)
    factor = clip_bound / jnp.maximum(jnp.sqrt(row), clip_bound)
    total = None
    for p in range(patients):
        total = add_to(total, sums[p] * factor[:, p : p + 1])
    rounded = total.astype(bf16)
    for j in range(pieces.shape[0]):
        pieces[j] = rounded


def update(pieces, weights, prev_state, tree_noise, state_next, weights_next, gathered):
    count, length, lanes = pieces.shape
    columns = state_next.shape[1]
    for j in range(count):
        gathered[j * length : (j + 1) * length, :] = pieces[j].astype(f32)
    for start in range(0, columns, 128):
        span = slice(start, min(start + 128, columns))
        combined = gathered[span, :].T
        state_next[:, span] = prev_state[:, span] + combined
        weights_next[:, span] = weights[:, span] - step_rate * (combined + tree_noise[:, span])


def exchange(rows):
    return lax.all_to_all(rows, "slab", 0, 0)


def per_device(features, cotangent, weights, prev_state, tree_noise):
    peers, patients = lax.axis_size("slab"), lax.axis_size("pat")
    devices = peers * patients
    slab = lax.axis_index("slab")
    own = features[0].transpose(1, 0, 2)
    cotan = cotangent[0].transpose(1, 0, 2)
    depth, channels, cells = own.shape
    cell_count = peers * depth * cells
    columns = weights.shape[2]

    def edge_planes(last):
        return jnp.concatenate(
            [
                lax.dynamic_slice_in_dim(own, jnp.where(last, depth - FEATURE_HALO, 0), FEATURE_HALO, 0),
                lax.dynamic_slice_in_dim(cotan, jnp.where(last, depth - COTAN_HALO, 0), COTAN_HALO, 0),
            ],
            axis=0,
        )

    even = slab % 2 == 0
    even_pairs = [(i, i ^ 1) for i in range(peers)]
    odd_pairs = [(i, (i + 1) % peers if i % 2 else (i - 1) % peers) for i in range(peers)]
    even_recv = lax.ppermute(edge_planes(even), "slab", even_pairs)
    odd_recv = lax.ppermute(edge_planes(~even), "slab", odd_pairs)

    stack_shape = sds((3 * channels, 9 * channels), bf16)
    kernel_one, kernel_two, kernel_back = call(kernel_stacks, (stack_shape,) * 3, weights)

    rows_shape = sds((peers, 2 * channels), f32)

    def scratch(planes):
        return [
            pltpu.VMEM((3 * channels, cells + 2 * PAD), bf16),
            pltpu.VMEM((9 * channels, planes * cells), bf16),
            pltpu.VMEM((3 * channels, planes * cells), f32),
        ]

    def field(planes, dtype):
        return sds((planes, channels, cells), dtype)

    conv_flops = 2 * 27 * channels * channels * cells * depth
    first, totals = call(
        functools.partial(first_conv, peers),
        (field(depth + 4, f32), rows_shape),
        own, even_recv, odd_recv, kernel_one,
        scratch=scratch(depth + 6), flops=conv_flops,
    )
    rows_one = exchange(totals)
    hidden, second, totals = call(
        functools.partial(second_conv, peers, cell_count),
        (field(depth + 2, bf16), field(depth + 2, f32), rows_shape),
        rows_one, first, kernel_two,
        scratch=scratch(depth + 4), flops=conv_flops,
    )
    rows_two = exchange(totals)
    gradient_two, totals = call(
        functools.partial(second_gradient, peers, cell_count),
        (field(depth + 2, f32), rows_shape),
        rows_two, second, cotan, even_recv, odd_recv,
    )
    rows_three = exchange(totals)
    cotan_two, gradient_one, totals = call(
        functools.partial(back_conv, peers, cell_count),
        (field(depth, bf16), field(depth, f32), rows_shape),
        rows_one, rows_two, rows_three, first, second, gradient_two, kernel_back,
        scratch=scratch(depth + 2), flops=conv_flops,
    )
    rows_four = exchange(totals)

    length = 8 * pl.cdiv(columns, 8 * devices)
    pieces_shape = sds((devices, length, 2 * channels), bf16)
    pieces = call(
        functools.partial(kernel_grads, peers, cell_count),
        pieces_shape,
        rows_one, rows_four, first, gradient_one, cotan_two, hidden, own, even_recv, odd_recv,
        scratch=[
            pltpu.VMEM((3 * channels, cells + 2 * PAD), bf16),
            pltpu.VMEM((9 * channels, (depth + 2) * cells), bf16),
            pltpu.VMEM((3 * channels, (depth + 2) * cells), bf16),
            pltpu.VMEM((devices * length, 2 * channels), f32),
        ],
        flops=2 * conv_flops,
    )
    pieces = lax.all_to_all(pieces, AXES, 0, 0)
    sums, squares = call(
        functools.partial(piece_sums, patients),
        (sds((patients, length, 2 * channels), f32), sds((devices, 128), f32)),
        pieces,
    )
    squares = lax.all_to_all(squares, AXES, 0, 0)
    pieces = call(functools.partial(clipped, patients), pieces_shape, squares, sums)
    pieces = lax.all_to_all(pieces, AXES, 0, 0)
    flat = (2 * channels, columns)
    state_next, weights_next = call(
        update,
        (sds(flat, f32), sds(flat, f32)),
        pieces, weights.reshape(flat), prev_state.reshape(flat), tree_noise.reshape(flat),
        scratch=[pltpu.VMEM((devices * length, 2 * channels), f32)],
    )
    return (state_next.reshape(weights.shape), weights_next.reshape(weights.shape))


def solution(mesh):
    return jax.shard_map(
        per_device,
        mesh=mesh,
        in_specs=(P("pat", None, "slab", None), P("pat", None, "slab", None), P(), P(), P()),
        out_specs=(P(), P()),
        check_vma=False,
    )
```

```python
import functools

import jax
import jax.numpy as jnp
from jax import lax
from jax.experimental import pallas as pl
from jax.experimental.pallas import tpu as pltpu
from jax.sharding import PartitionSpec as P


W = 24

eps_norm = 1e-05
clip_bound = 400.0
step_rate = 0.1

f32 = jnp.float32
bf16 = jnp.bfloat16

AXES = ("pat", "slab")
PAD = 128
FEATURE_HALO = 3
COTAN_HALO = 1


def call(kernel, out_shape, *args, scratch=(), flops=0):
    vmem = pl.BlockSpec(memory_space=pltpu.VMEM)
    size = sum(a.size * a.dtype.itemsize for a in args)
    return pl.pallas_call(
        kernel,
        out_shape=out_shape,
        in_specs=[vmem] * len(args),
        out_specs=jax.tree.map(lambda _: vmem, out_shape),
        scratch_shapes=list(scratch),
        cost_estimate=pl.CostEstimate(flops=flops, bytes_accessed=size, transcendentals=0),
        compiler_params=pltpu.CompilerParams(vmem_limit_bytes=14 * 2**20),
    )(*args)


def sds(shape, dtype):
    return jax.ShapeDtypeStruct(shape, dtype)


def column_masks(cells):
    column = lax.broadcasted_iota(jnp.int32, (1, cells), 1) % W
    return (column != W - 1).astype(bf16), (column != 0).astype(bf16)


def patches(plane, edge, stack, z):
    channels, cells = plane.shape
    not_last, not_first = column_masks(cells)
    edge[0:channels, PAD + 1 : PAD + 1 + cells] = plane * not_last
    edge[channels : 2 * channels, PAD : PAD + cells] = plane
    edge[2 * channels : 3 * channels, PAD - 1 : PAD - 1 + cells] = plane * not_first
    for b in range(3):
        start = PAD + (b - 1) * W
        stack[b * 3 * channels : (b + 1) * 3 * channels, z * cells : (z + 1) * cells] = edge[
            :, start : start + cells
        ]


def products(planes, kernel, edges, stack, product):
    edges[...] = jnp.zeros_like(edges)
    count = len(planes)

    def fill(z):
        plane = planes[z]() if callable(planes[z]) else planes[z]
        patches(plane, edges.at[z % 2], stack, z)
        return plane.shape[1]

    cells = fill(0)
    if count > 1:
        fill(1)
    for z in range(0, count, 2):
        for ahead in range(z + 2, min(z + 4, count)):
            fill(ahead)
        span = slice(z * cells, min(z + 2, count) * cells)
        product[:, span] = jnp.dot(kernel[...], stack[:, span], preferred_element_type=f32)


def tap(product, a, z, channels, cells):
    return product[a * channels : (a + 1) * channels, z * cells : (z + 1) * cells]


def depth_sum(product, z, channels, cells):
    return (
        tap(product, 0, z, channels, cells)
        + tap(product, 1, z + 1, channels, cells)
        + tap(product, 2, z + 2, channels, cells)
    )


def eye(size):
    return lax.broadcasted_iota(jnp.int32, (size, size), 0) == lax.broadcasted_iota(
        jnp.int32, (size, size), 1
    )


def to_row(first, second):
    both = jnp.concatenate([first, second], axis=0)
    size = both.shape[0]
    return jnp.sum(jnp.where(eye(size), both, 0.0), axis=0, keepdims=True)


def to_columns(rows):
    row = jnp.sum(rows, axis=0, keepdims=True)
    size = row.shape[1]
    both = jnp.sum(jnp.where(eye(size), row, 0.0), axis=1, keepdims=True)
    return both[: size // 2], both[size // 2 :]


def moments(rows, cell_count):
    totals, squares = to_columns(rows)
    centre = totals / cell_count
    return centre, lax.rsqrt(squares / cell_count - centre * centre + eps_norm)


def sigmoid(values):
    return 1.0 / (1.0 + jnp.exp(-values))


def slope(values):
    gate = sigmoid(values)
    return gate * (1.0 + values * (1.0 - gate))


def add_to(total, value):
    return value if total is None else total + value


def send_totals(ref, first, second):
    row = to_row(
        jnp.sum(first, axis=1, keepdims=True), jnp.sum(second, axis=1, keepdims=True)
    )
    ref[...] = jnp.broadcast_to(row, ref.shape)


def inside(z, halo, depth, slab, peers, value):
    if z < halo:
        return jnp.where(slab > 0, value, jnp.zeros_like(value))
    if z >= halo + depth:
        return jnp.where(slab < peers - 1, value, jnp.zeros_like(value))
    return value


def cut_edges(own, cotan, near_even, near_odd, far_even, far_odd, sems):
    depth = own.shape[0]
    even = lax.axis_index("slab") % 2 == 0
    copies = []

    def copy(source, start, count, target, at):
        copies.append(
            pltpu.make_async_copy(
                source.at[pl.ds(start, count)], target.at[pl.ds(at, count)], sems.at[len(copies)]
            )
        )

    for near, far, last in ((near_even, far_even, even), (near_odd, far_odd, ~even)):
        copy(own, jnp.where(last, depth - 1, 0), 1, near, 0)
        copy(own, jnp.where(last, depth - FEATURE_HALO, 1), FEATURE_HALO - 1, far, 0)
        copy(cotan, jnp.where(last, depth - 1, 0), 1, far, FEATURE_HALO - 1)
    for c in copies:
        c.start()
    for c in copies:
        c.wait()


def halo_plane(even_recv, odd_recv, z, before, slab, peers):
    even = slab % 2 == 0
    picked = jnp.where(even == before, odd_recv[z], even_recv[z])
    return jnp.where(slab == (0 if before else peers - 1), jnp.zeros_like(picked), picked)


def kernel_stack(rounded, target):
    channels = rounded.shape[0]
    width = 9 * channels
    for a in range(3):
        target[a * channels : (a + 1) * channels, :] = rounded[:, a * width : (a + 1) * width]


def own_products(weights, own, kernel, kernel_two, back, stack, product, edge):
    channels = weights.shape[1]
    kernel_stack(weights[0].astype(bf16), kernel)
    products([own[z] for z in range(own.shape[0])], kernel, edge, stack, product)
    kernel_stack(weights[1].astype(bf16), kernel_two)
    turned = weights[1].T
    for a in range(3):
        for tap_at in range(9):
            block = (2 - a) * 9 + 8 - tap_at
            back[
                a * channels : (a + 1) * channels, tap_at * channels : (tap_at + 1) * channels
            ] = turned[block * channels : (block + 1) * channels, :].astype(bf16)


def first_conv(peers, near_even, near_odd, kernel, own_product, first, totals, stack, product, edge):
    slab = lax.axis_index("slab")
    depth, channels, cells = first.shape
    planes = [halo_plane(near_even, near_odd, 0, before, slab, peers) for before in (True, False)]
    products(planes, kernel, edge, stack, product)

    def part(a, z):
        if 0 <= z < depth:
            return tap(own_product, a, z, channels, cells)
        return tap(product, a, 0 if z < 0 else 1, channels, cells)

    s = q = None
    for z in range(depth):
        value = part(0, z - 1) + part(1, z) + part(2, z + 1)
        first[z] = value
        s, q = add_to(s, value), add_to(q, value * value)
    send_totals(totals, s, q)


def first_conv_edges(peers, far_even, far_odd, kernel, own_product, near_product, stack, product, edge):
    slab = lax.axis_index("slab")
    cells = stack.shape[1] // 4
    channels = own_product.shape[0] // 3
    depth = own_product.shape[1] // cells
    planes = [
        halo_plane(far_even, far_odd, z, before, slab, peers) for before in (True, False) for z in (0, 1)
    ]
    products(planes, kernel, edge, stack, product)
    where = {-3: 0, -2: 1, depth + 1: 2, depth + 2: 3}

    def part(a, z):
        if 0 <= z < depth:
            return tap(own_product, a, z, channels, cells)
        if z in (-1, depth):
            return tap(near_product, a, 0 if z < 0 else 1, channels, cells)
        return tap(product, a, where[z], channels, cells)

    return [part(0, z - 1) + part(1, z) + part(2, z + 1) for z in (-2, -1, depth, depth + 1)]


def second_conv(
    peers, cell_count, rows, first, far_even, far_odd, kernel_one, own_product, near_product, kernel,
    second, totals, stack, product, far_stack, far_product, edge,
):
    edges = first_conv_edges(
        peers, far_even, far_odd, kernel_one, own_product, near_product, far_stack, far_product, edge
    )
    slab = lax.axis_index("slab")
    depth, channels, cells = first.shape
    centre, spread = moments(rows[...], cell_count)

    def plane(z):
        at = z - 2
        source = first[at] if 0 <= at < depth else edges[z if z < 2 else z - depth]
        normed = (source - centre) * spread
        return inside(z, 2, depth, slab, peers, (normed * sigmoid(normed)).astype(bf16))

    products([functools.partial(plane, z) for z in range(depth + 4)], kernel, edge, stack, product)
    s = q = None
    for z in range(depth + 2):
        value = depth_sum(product, z, channels, cells)
        second[z] = value
        if 1 <= z < depth + 1:
            s, q = add_to(s, value), add_to(q, value * value)
    send_totals(totals, s, q)


def second_gradient(peers, cell_count, rows, second, cotan, far_even, far_odd, gradient, totals):
    slab = lax.axis_index("slab")
    depth = cotan.shape[0]
    centre, spread = moments(rows[...], cell_count)
    s = q = None
    for z in range(depth + 2):
        if 1 <= z < depth + 1:
            upstream = cotan[z - 1]
        else:
            upstream = halo_plane(far_even, far_odd, FEATURE_HALO - 1, z == 0, slab, peers)
        normed = (second[z] - centre) * spread
        value = upstream.astype(f32) * slope(normed)
        gradient[z] = value
        if 1 <= z < depth + 1:
            s, q = add_to(s, value), add_to(q, value * normed)
    send_totals(totals, s, q)


def back_conv(
    peers, cell_count, rows_one, rows_two, rows, first, second, gradient, kernel,
    cotan_two, gradient_one, normed_one, totals, edge, stack, product,
):
    slab = lax.axis_index("slab")
    extended, channels, cells = second.shape
    depth = extended - 2
    centre, spread = moments(rows_two[...], cell_count)
    mean, crossed = (x / cell_count for x in to_columns(rows[...]))

    def plane(z):
        normed = (second[z] - centre) * spread
        value = (spread * (gradient[z] - mean - normed * crossed)).astype(bf16)
        value = inside(z, 1, depth, slab, peers, value)
        if 1 <= z < depth + 1:
            cotan_two[z - 1] = value
        return value

    products([functools.partial(plane, z) for z in range(extended)], kernel, edge, stack, product)
    centre, spread = moments(rows_one[...], cell_count)
    s = q = None
    for z in range(depth):
        normed = (first[z] - centre) * spread
        normed_one[z] = normed
        value = depth_sum(product, z, channels, cells) * slope(normed)
        gradient_one[z] = value
        s, q = add_to(s, value), add_to(q, value * normed)
    send_totals(totals, s, q)


def fill_taps(cotans, taps, first, count):
    depth, (channels, cells) = len(cotans), cotans[0].shape
    zero = jnp.zeros((channels, cells), bf16)
    for a in range(3):
        for z in range(first, first + count):
            taps[a * channels : (a + 1) * channels, z * cells : (z + 1) * cells] = (
                cotans[z - a] if 0 <= z - a < depth else zero
            )


def contract(stack, taps):
    return lax.dot_general(stack, taps, (((1,), (1,)), ((), ())), preferred_element_type=f32)


def kernel_grads(
    cell_count, rows_one, rows, normed_one, gradient_one, own_stack, near_stack, cotan_two, hidden_stack,
    pieces, taps, taps_two, gathered,
):
    depth, channels, cells = normed_one.shape
    count, length, _ = pieces.shape
    _, spread = moments(rows_one[...], cell_count)
    mean, crossed = (x / cell_count for x in to_columns(rows[...]))
    cotans = [
        (spread * (gradient_one[z] - mean - normed_one[z] * crossed)).astype(bf16) for z in range(depth)
    ]
    fill_taps(cotans, taps, 0, depth + 2)
    width = 9 * channels
    own_taps = taps[:, cells : (depth + 1) * cells]
    near_taps = jnp.concatenate([taps[:, :cells], taps[:, (depth + 1) * cells :]], axis=1)
    grad_one = contract(own_stack[...], own_taps) + contract(near_stack[...], near_taps)
    fill_taps([cotan_two[z] for z in range(depth)], taps_two, 0, depth + 2)
    grad_two = contract(hidden_stack[:, cells : (depth + 3) * cells], taps_two[...])
    for a in range(3):
        span = slice(a * channels, (a + 1) * channels)
        rows_of = slice(a * width, (a + 1) * width)
        gathered[rows_of, :channels] = grad_one[:, span]
        gathered[rows_of, channels:] = grad_two[:, span]
    if count * length > 3 * width:
        gathered[3 * width :, :] = jnp.zeros((count * length - 3 * width, 2 * channels), f32)
    for j in range(count):
        pieces[j] = gathered[j * length : (j + 1) * length, :].astype(bf16)


def piece_sums(patients, pieces, sums, squares):
    count, _, _ = pieces.shape
    peers = count // patients
    lane = lax.broadcasted_iota(jnp.int32, (1, squares.shape[1]), 1)
    row = jnp.zeros((1, squares.shape[1]), f32)
    for p in range(patients):
        total = None
        for j in range(peers):
            total = add_to(total, pieces[p * peers + j].astype(f32))
        sums[p] = total
        part = jnp.sum(jnp.sum(total * total, axis=0, keepdims=True), axis=1, keepdims=True)
        row = jnp.where(lane == p, part, row)
    squares[...] = jnp.broadcast_to(row, squares.shape)


def clipped(patients, squares, sums, pieces):
    row = jnp.sum(squares[...], axis=0, keepdims=True)
    factor = clip_bound / jnp.maximum(jnp.sqrt(row), clip_bound)
    total = None
    for p in range(patients):
        total = add_to(total, sums[p] * factor[:, p : p + 1])
    rounded = total.astype(bf16)
    for j in range(pieces.shape[0]):
        pieces[j] = rounded


def update(pieces, weights, prev_state, tree_noise, state_next, weights_next, gathered):
    count, length, _ = pieces.shape
    columns = state_next.shape[1]
    for j in range(count):
        gathered[j * length : (j + 1) * length, :] = pieces[j].astype(f32)
    for start in range(0, columns, 128):
        span = slice(start, min(start + 128, columns))
        combined = gathered[span, :].T
        state_next[:, span] = prev_state[:, span] + combined
        weights_next[:, span] = weights[:, span] - step_rate * (combined + tree_noise[:, span])


def trade(planes, pairs):
    return lax.ppermute(planes, "slab", pairs)


def exchange(rows):
    return lax.all_to_all(rows, "slab", 0, 0)


def per_device(features, cotangent, weights, prev_state, tree_noise):
    peers, patients = lax.axis_size("slab"), lax.axis_size("pat")
    devices = peers * patients
    own = features[0].transpose(1, 0, 2)
    cotan = cotangent[0].transpose(1, 0, 2)
    depth, channels, cells = own.shape
    cell_count = peers * depth * cells
    columns = weights.shape[2]
    rows_shape = sds((peers, 2 * channels), f32)
    edge = pltpu.VMEM((2, 3 * channels, cells + 2 * PAD), bf16)

    def field(planes, dtype):
        return sds((planes, channels, cells), dtype)

    def stack_of(planes):
        return sds((9 * channels, planes * cells), bf16)

    def product_of(planes):
        return sds((3 * channels, planes * cells), f32)

    def scratch_of(shape):
        return pltpu.VMEM(shape.shape, shape.dtype)

    def flops(planes):
        return 2 * 27 * channels * channels * cells * planes

    far = field(FEATURE_HALO - 1 + COTAN_HALO, bf16)
    near_even, near_odd, far_even, far_odd = pl.pallas_call(
        cut_edges,
        out_shape=(field(1, bf16), field(1, bf16), far, far),
        in_specs=[pl.BlockSpec(memory_space=pltpu.HBM)] * 2,
        out_specs=(pl.BlockSpec(memory_space=pltpu.VMEM),) * 4,
        scratch_shapes=[pltpu.SemaphoreType.DMA((6,))],
        compiler_params=pltpu.CompilerParams(vmem_limit_bytes=2 * 2**20),
    )(own, cotan)
    even_pairs = [(i, i ^ 1) for i in range(peers)]
    odd_pairs = [(i, (i + 1) % peers if i % 2 else (i - 1) % peers) for i in range(peers)]
    near_even = trade(near_even, even_pairs)
    near_odd = trade(near_odd, odd_pairs)
    far_even = trade(far_even, even_pairs)
    far_odd = trade(far_odd, odd_pairs)

    kernel_shape = sds((3 * channels, 9 * channels), bf16)
    kernel_one, kernel_two, kernel_back, own_stack, own_product = call(
        own_products,
        (kernel_shape, kernel_shape, kernel_shape, stack_of(depth), product_of(depth)),
        weights, own,
        scratch=[edge], flops=flops(depth),
    )
    first, totals, near_stack, near_product = call(
        functools.partial(first_conv, peers),
        (field(depth, f32), rows_shape, stack_of(2), product_of(2)),
        near_even, near_odd, kernel_one, own_product,
        scratch=[edge], flops=flops(2),
    )
    rows_one = exchange(totals)
    second, totals, hidden_stack = call(
        functools.partial(second_conv, peers, cell_count),
        (field(depth + 2, f32), rows_shape, stack_of(depth + 4)),
        rows_one, first, far_even, far_odd, kernel_one, own_product, near_product, kernel_two,
        scratch=[scratch_of(product_of(depth + 4)), scratch_of(stack_of(4)), scratch_of(product_of(4)), edge],
        flops=flops(depth + 4),
    )
    rows_two = exchange(totals)
    gradient_two, totals = call(
        functools.partial(second_gradient, peers, cell_count),
        (field(depth + 2, f32), rows_shape),
        rows_two, second, cotan, far_even, far_odd,
    )
    rows_three = exchange(totals)
    cotan_two, gradient_one, normed_one, totals = call(
        functools.partial(back_conv, peers, cell_count),
        (field(depth, bf16), field(depth, f32), field(depth, f32), rows_shape),
        rows_one, rows_two, rows_three, first, second, gradient_two, kernel_back,
        scratch=[edge, scratch_of(stack_of(depth + 2)), scratch_of(product_of(depth + 2))],
        flops=flops(depth + 2),
    )
    rows_four = exchange(totals)
    taps = pltpu.VMEM((3 * channels, (depth + 2) * cells), bf16)

    length = 8 * pl.cdiv(columns, 8 * devices)
    pieces_shape = sds((devices, length, 2 * channels), bf16)
    pieces = call(
        functools.partial(kernel_grads, cell_count),
        pieces_shape,
        rows_one, rows_four, normed_one, gradient_one, own_stack, near_stack, cotan_two, hidden_stack,
        scratch=[taps, taps, pltpu.VMEM((devices * length, 2 * channels), f32)],
        flops=flops(depth + 2),
    )
    pieces = lax.all_to_all(pieces, AXES, 0, 0)
    sums, squares = call(
        functools.partial(piece_sums, patients),
        (sds((patients, length, 2 * channels), f32), sds((devices, 128), f32)),
        pieces,
    )
    squares = lax.all_to_all(squares, AXES, 0, 0)
    pieces = call(functools.partial(clipped, patients), pieces_shape, squares, sums)
    pieces = lax.all_to_all(pieces, AXES, 0, 0)
    flat = (2 * channels, columns)
    state_next, weights_next = call(
        update,
        (sds(flat, f32), sds(flat, f32)),
        pieces, weights.reshape(flat), prev_state.reshape(flat), tree_noise.reshape(flat),
        scratch=[pltpu.VMEM((devices * length, 2 * channels), f32)],
    )
    return (state_next.reshape(weights.shape), weights_next.reshape(weights.shape))


def solution(mesh):
    return jax.shard_map(
        per_device,
        mesh=mesh,
        in_specs=(P("pat", None, "slab", None), P("pat", None, "slab", None), P(), P(), P()),
        out_specs=(P(), P()),
        check_vma=False,
    )
```

```python
import functools

import jax
import jax.numpy as jnp
from jax import lax
from jax.experimental import pallas as pl
from jax.experimental.pallas import tpu as pltpu
from jax.sharding import PartitionSpec as P


W = 24

eps_norm = 1e-05
clip_bound = 400.0
step_rate = 0.1

f32 = jnp.float32
bf16 = jnp.bfloat16

AXES = ("pat", "slab")
FEATURE_HALO = 3
COTAN_HALO = 1
EARLY = 10**10


def call(kernel, out_shape, *args, scratch=(), flops=0):
    vmem = pl.BlockSpec(memory_space=pltpu.VMEM)
    size = sum(a.size * a.dtype.itemsize for a in args)
    return pl.pallas_call(
        kernel,
        out_shape=out_shape,
        in_specs=[vmem] * len(args),
        out_specs=jax.tree.map(lambda _: vmem, out_shape),
        scratch_shapes=list(scratch),
        cost_estimate=pl.CostEstimate(flops=flops, bytes_accessed=size, transcendentals=0),
        compiler_params=pltpu.CompilerParams(vmem_limit_bytes=18 * 2**20),
    )(*args)


def sds(shape, dtype):
    return jax.ShapeDtypeStruct(shape, dtype)


def patches(plane, stack, z):
    channels, cells = plane.shape
    column = lax.broadcasted_iota(jnp.int32, (1, cells), 1) % W
    span = slice(z * cells, (z + 1) * cells)
    stack[0:channels, span] = pltpu.roll(plane, 1, 1) * (column != 0).astype(bf16)
    stack[channels : 2 * channels, span] = plane
    stack[2 * channels : 3 * channels, span] = pltpu.roll(plane, cells - 1, 1) * (
        column != W - 1
    ).astype(bf16)


def products(planes, kernel, stack, product):
    count = len(planes)

    def fill(z):
        plane = planes[z]() if callable(planes[z]) else planes[z]
        patches(plane, stack, z)
        return plane.shape[1]

    cells = fill(0)
    if count > 1:
        fill(1)
    for z in range(0, count, 2):
        for ahead in range(z + 2, min(z + 4, count)):
            fill(ahead)
        span = slice(z * cells, min(z + 2, count) * cells)
        product[:, span] = jnp.dot(kernel[...], stack[:, span], preferred_element_type=f32)


def tap(product, a, b, z, channels, cells):
    at = 3 * a + b
    return product[at * channels : (at + 1) * channels, z * cells : (z + 1) * cells]


def row_shift(value, rows):
    if rows == 0:
        return value
    cells = value.shape[1]
    cell = lax.broadcasted_iota(jnp.int32, (1, cells), 1)
    kept = cell < cells - W if rows > 0 else cell >= W
    moved = pltpu.roll(value, (-rows * W) % cells, 1)
    if value.dtype == bf16:
        return moved * kept.astype(bf16)
    return jnp.where(kept, moved, 0.0)


def tap_sum(part, z):
    total = None
    for b in range(3):
        rows = part(0, b, z - 1) + part(1, b, z) + part(2, b, z + 1)
        total = add_to(total, row_shift(rows, b - 1))
    return total


def depth_sum(product, z, channels, cells):
    return tap_sum(lambda a, b, at: tap(product, a, b, at + 1, channels, cells), z)


def eye(size):
    return lax.broadcasted_iota(jnp.int32, (size, size), 0) == lax.broadcasted_iota(
        jnp.int32, (size, size), 1
    )


def to_row(first, second):
    both = jnp.concatenate([first, second], axis=0)
    size = both.shape[0]
    return jnp.sum(jnp.where(eye(size), both, 0.0), axis=0, keepdims=True)


def to_columns(rows):
    row = jnp.sum(rows, axis=0, keepdims=True)
    size = row.shape[1]
    both = jnp.sum(jnp.where(eye(size), row, 0.0), axis=1, keepdims=True)
    return both[: size // 2], both[size // 2 :]


def moments(rows, cell_count):
    totals, squares = to_columns(rows)
    centre = totals / cell_count
    return centre, lax.rsqrt(squares / cell_count - centre * centre + eps_norm)


def sigmoid(values):
    return 1.0 / (1.0 + jnp.exp(-values))


def slope(values):
    gate = sigmoid(values)
    return gate * (1.0 + values * (1.0 - gate))


def add_to(total, value):
    return value if total is None else total + value


def send_totals(ref, first, second):
    row = to_row(
        jnp.sum(first, axis=1, keepdims=True), jnp.sum(second, axis=1, keepdims=True)
    )
    ref[...] = jnp.broadcast_to(row, ref.shape)


def inside(z, halo, depth, slab, peers, value):
    if z < halo:
        return jnp.where(slab > 0, value, jnp.zeros_like(value))
    if z >= halo + depth:
        return jnp.where(slab < peers - 1, value, jnp.zeros_like(value))
    return value


def cut_near(own, near_even, near_odd):
    depth = own.shape[0]
    even = lax.axis_index("slab") % 2 == 0
    for near, last in ((near_even, even), (near_odd, ~even)):
        near[0] = own[jnp.where(last, depth - 1, 0)]


def cut_far(own, cotan, far_even, far_odd):
    depth = own.shape[0]
    even = lax.axis_index("slab") % 2 == 0
    for far, last in ((far_even, even), (far_odd, ~even)):
        for z in range(FEATURE_HALO - 1):
            far[z] = own[jnp.where(last, depth - FEATURE_HALO, 1) + z]
        far[FEATURE_HALO - 1] = cotan[jnp.where(last, depth - 1, 0)]


def halo_plane(even_recv, odd_recv, z, before, slab, peers):
    even = slab % 2 == 0
    picked = jnp.where(even == before, odd_recv[z], even_recv[z])
    return jnp.where(slab == (0 if before else peers - 1), jnp.zeros_like(picked), picked)


def kernel_stack(rounded, target):
    channels = rounded.shape[0]
    width = 3 * channels
    for at in range(9):
        target[at * channels : (at + 1) * channels, :] = rounded[:, at * width : (at + 1) * width]


def own_products(weights, own, kernel, kernel_two, back, stack, product):
    channels = weights.shape[1]
    kernel_stack(weights[0].astype(bf16), kernel)
    products([own[z] for z in range(own.shape[0])], kernel, stack, product)
    kernel_stack(weights[1].astype(bf16), kernel_two)
    turned = weights[1].T
    for at in range(9):
        for e in range(3):
            block = (8 - at) * 3 + 2 - e
            back[at * channels : (at + 1) * channels, e * channels : (e + 1) * channels] = turned[
                block * channels : (block + 1) * channels, :
            ].astype(bf16)


def first_conv(peers, near_even, near_odd, kernel, own_product, first, totals, stack, product):
    slab = lax.axis_index("slab")
    depth, channels, cells = first.shape
    planes = [halo_plane(near_even, near_odd, 0, before, slab, peers) for before in (True, False)]
    products(planes, kernel, stack, product)

    def part(a, b, z):
        if 0 <= z < depth:
            return tap(own_product, a, b, z, channels, cells)
        return tap(product, a, b, 0 if z < 0 else 1, channels, cells)

    s = q = None
    for z in range(depth):
        value = tap_sum(part, z)
        first[z] = value
        s, q = add_to(s, value), add_to(q, value * value)
    send_totals(totals, s, q)


def first_conv_edges(peers, far_even, far_odd, kernel, own_product, near_product, stack, product):
    slab = lax.axis_index("slab")
    cells = stack.shape[1] // 4
    channels = own_product.shape[0] // 9
    depth = own_product.shape[1] // cells
    planes = [
        halo_plane(far_even, far_odd, z, before, slab, peers) for before in (True, False) for z in (0, 1)
    ]
    products(planes, kernel, stack, product)
    where = {-3: 0, -2: 1, depth + 1: 2, depth + 2: 3}

    def part(a, b, z):
        if 0 <= z < depth:
            return tap(own_product, a, b, z, channels, cells)
        if z in (-1, depth):
            return tap(near_product, a, b, 0 if z < 0 else 1, channels, cells)
        return tap(product, a, b, where[z], channels, cells)

    return [tap_sum(part, z) for z in (-2, -1, depth, depth + 1)]


def second_conv(
    peers, cell_count, rows, first, far_even, far_odd, kernel_one, own_product, near_product, kernel,
    second, totals, stack, product, far_stack, far_product,
):
    edges = first_conv_edges(
        peers, far_even, far_odd, kernel_one, own_product, near_product, far_stack, far_product
    )
    slab = lax.axis_index("slab")
    depth, channels, cells = first.shape
    centre, spread = moments(rows[...], cell_count)

    def plane(z):
        at = z - 2
        source = first[at] if 0 <= at < depth else edges[z if z < 2 else z - depth]
        normed = (source - centre) * spread
        return inside(z, 2, depth, slab, peers, (normed * sigmoid(normed)).astype(bf16))

    products([functools.partial(plane, z) for z in range(depth + 4)], kernel, stack, product)
    s = q = None
    for z in range(depth + 2):
        value = depth_sum(product, z, channels, cells)
        second[z] = value
        if 1 <= z < depth + 1:
            s, q = add_to(s, value), add_to(q, value * value)
    send_totals(totals, s, q)


def second_gradient(peers, cell_count, rows, second, cotan, far_even, far_odd, gradient, totals):
    slab = lax.axis_index("slab")
    depth = cotan.shape[0]
    centre, spread = moments(rows[...], cell_count)
    s = q = None
    for z in range(depth + 2):
        if 1 <= z < depth + 1:
            upstream = cotan[z - 1]
        else:
            upstream = halo_plane(far_even, far_odd, FEATURE_HALO - 1, z == 0, slab, peers)
        normed = (second[z] - centre) * spread
        value = upstream.astype(f32) * slope(normed)
        gradient[z] = value
        if 1 <= z < depth + 1:
            s, q = add_to(s, value), add_to(q, value * normed)
    send_totals(totals, s, q)


def back_conv(
    peers, cell_count, rows_one, rows_two, rows, first, second, gradient, kernel,
    cotan_two, gradient_one, normed_one, totals, stack, product,
):
    slab = lax.axis_index("slab")
    extended, channels, cells = second.shape
    depth = extended - 2
    centre, spread = moments(rows_two[...], cell_count)
    mean, crossed = (x / cell_count for x in to_columns(rows[...]))

    def plane(z):
        normed = (second[z] - centre) * spread
        value = (spread * (gradient[z] - mean - normed * crossed)).astype(bf16)
        value = inside(z, 1, depth, slab, peers, value)
        if 1 <= z < depth + 1:
            cotan_two[z - 1] = value
        return value

    products([functools.partial(plane, z) for z in range(extended)], kernel, stack, product)
    centre, spread = moments(rows_one[...], cell_count)
    s = q = None
    for z in range(depth):
        normed = (first[z] - centre) * spread
        normed_one[z] = normed
        value = depth_sum(product, z, channels, cells) * slope(normed)
        gradient_one[z] = value
        s, q = add_to(s, value), add_to(q, value * normed)
    send_totals(totals, s, q)


def fill_taps(cotans, taps):
    depth, (channels, cells) = len(cotans), cotans[0].shape
    zero = jnp.zeros((3 * channels, cells), bf16)
    for a in range(3):
        for z in range(depth + 2):
            if not 0 <= z - a < depth:
                taps[3 * a * channels : 3 * (a + 1) * channels, z * cells : (z + 1) * cells] = zero
    for z, plane in enumerate(cotans):
        for b in range(3):
            value = row_shift(plane, 1 - b)
            for a in range(3):
                at = 3 * a + b
                taps[at * channels : (at + 1) * channels, (z + a) * cells : (z + a + 1) * cells] = value


def contract(taps, stack):
    return lax.dot_general(taps, stack, (((1,), (1,)), ((), ())), preferred_element_type=f32)


def kernel_grads(
    cell_count, rows_one, rows, normed_one, gradient_one, own_stack, near_stack, cotan_two, hidden_stack,
    pieces, taps, taps_two, gathered,
):
    depth, channels, cells = normed_one.shape
    count, length, _ = pieces.shape
    _, spread = moments(rows_one[...], cell_count)
    mean, crossed = (x / cell_count for x in to_columns(rows[...]))
    cotans = [
        (spread * (gradient_one[z] - mean - normed_one[z] * crossed)).astype(bf16) for z in range(depth)
    ]
    fill_taps(cotans, taps)
    width = 9 * channels
    own_taps = taps[:, cells : (depth + 1) * cells]
    near_taps = jnp.concatenate([taps[:, :cells], taps[:, (depth + 1) * cells :]], axis=1)
    grad_one = contract(own_taps, own_stack[...]) + contract(near_taps, near_stack[...])
    fill_taps([cotan_two[z] for z in range(depth)], taps_two)
    grad_two = contract(taps_two[...], hidden_stack[:, cells : (depth + 3) * cells])
    for e in range(3):
        span = slice(e * channels, (e + 1) * channels)
        rows_of = slice(e * width, (e + 1) * width)
        gathered[rows_of, :channels] = grad_one[:, span]
        gathered[rows_of, channels:] = grad_two[:, span]
    if count * length > 3 * width:
        gathered[3 * width :, :] = jnp.zeros((count * length - 3 * width, 2 * channels), f32)
    for j in range(count):
        pieces[j] = gathered[j * length : (j + 1) * length, :].astype(bf16)


def piece_sums(patients, pieces, sums, squares):
    count, _, _ = pieces.shape
    peers = count // patients
    lane = lax.broadcasted_iota(jnp.int32, (1, squares.shape[1]), 1)
    row = jnp.zeros((1, squares.shape[1]), f32)
    for p in range(patients):
        total = None
        for j in range(peers):
            total = add_to(total, pieces[p * peers + j].astype(f32))
        sums[p] = total
        part = jnp.sum(jnp.sum(total * total, axis=0, keepdims=True), axis=1, keepdims=True)
        row = jnp.where(lane == p, part, row)
    squares[...] = jnp.broadcast_to(row, squares.shape)


def clipped(patients, squares, sums, pieces):
    row = jnp.sum(squares[...], axis=0, keepdims=True)
    factor = clip_bound / jnp.maximum(jnp.sqrt(row), clip_bound)
    total = None
    for p in range(patients):
        total = add_to(total, sums[p] * factor[:, p : p + 1])
    rounded = total.astype(bf16)
    for j in range(pieces.shape[0]):
        pieces[j] = rounded


def update(pieces, weights, prev_state, tree_noise, state_next, weights_next, gathered):
    count, length, lanes = pieces.shape
    channels, blocks = lanes // 2, 27
    for j in range(count):
        gathered[j * length : (j + 1) * length, :] = pieces[j].astype(f32)

    def block(at, k):
        row = (at % 3 * 9 + at // 3) * channels
        return gathered[row : row + channels, k * channels : (k + 1) * channels]

    for at in range(0, blocks, 2):
        group = range(at, min(at + 2, blocks))
        span = slice(at * channels, (group[-1] + 1) * channels)
        for k in range(2):
            rows = slice(k * channels, (k + 1) * channels)
            combined = jnp.concatenate([block(i, k) for i in group], axis=1)
            state_next[rows, span] = prev_state[rows, span] + combined
            weights_next[rows, span] = weights[rows, span] - step_rate * (combined + tree_noise[rows, span])


def trade(planes, pairs):
    return lax.ppermute(planes, "slab", pairs)


def exchange(rows):
    return lax.all_to_all(rows, "slab", 0, 0)


def per_device(features, cotangent, weights, prev_state, tree_noise):
    peers, patients = lax.axis_size("slab"), lax.axis_size("pat")
    devices = peers * patients
    own = features[0].transpose(1, 0, 2)
    cotan = cotangent[0].transpose(1, 0, 2)
    depth, channels, cells = own.shape
    cell_count = peers * depth * cells
    columns = weights.shape[2]
    rows_shape = sds((peers, 2 * channels), f32)

    def field(planes, dtype):
        return sds((planes, channels, cells), dtype)

    def stack_of(planes):
        return sds((3 * channels, planes * cells), bf16)

    def product_of(planes):
        return sds((9 * channels, planes * cells), f32)

    def scratch_of(shape):
        return pltpu.VMEM(shape.shape, shape.dtype)

    def flops(planes):
        return 2 * 27 * channels * channels * cells * planes

    far = field(FEATURE_HALO - 1 + COTAN_HALO, bf16)
    near_even, near_odd = call(cut_near, (field(1, bf16),) * 2, own, flops=EARLY)
    far_even, far_odd = call(cut_far, (far,) * 2, own, cotan)
    even_pairs = [(i, i ^ 1) for i in range(peers)]
    odd_pairs = [(i, (i + 1) % peers if i % 2 else (i - 1) % peers) for i in range(peers)]
    near_even = trade(near_even, even_pairs)
    near_odd = trade(near_odd, odd_pairs)
    far_even = trade(far_even, even_pairs)
    far_odd = trade(far_odd, odd_pairs)

    kernel_shape = sds((9 * channels, 3 * channels), bf16)
    kernel_one, kernel_two, kernel_back, own_stack, own_product = call(
        own_products,
        (kernel_shape, kernel_shape, kernel_shape, stack_of(depth), product_of(depth)),
        weights, own,
        flops=flops(depth),
    )
    first, totals, near_stack, near_product = call(
        functools.partial(first_conv, peers),
        (field(depth, f32), rows_shape, stack_of(2), product_of(2)),
        near_even, near_odd, kernel_one, own_product,
        flops=flops(2),
    )
    rows_one = exchange(totals)
    second, totals, hidden_stack = call(
        functools.partial(second_conv, peers, cell_count),
        (field(depth + 2, f32), rows_shape, stack_of(depth + 4)),
        rows_one, first, far_even, far_odd, kernel_one, own_product, near_product, kernel_two,
        scratch=[scratch_of(product_of(depth + 4)), scratch_of(stack_of(4)), scratch_of(product_of(4))],
        flops=flops(depth + 4),
    )
    rows_two = exchange(totals)
    gradient_two, totals = call(
        functools.partial(second_gradient, peers, cell_count),
        (field(depth + 2, f32), rows_shape),
        rows_two, second, cotan, far_even, far_odd,
    )
    rows_three = exchange(totals)
    cotan_two, gradient_one, normed_one, totals = call(
        functools.partial(back_conv, peers, cell_count),
        (field(depth, bf16), field(depth, f32), field(depth, f32), rows_shape),
        rows_one, rows_two, rows_three, first, second, gradient_two, kernel_back,
        scratch=[scratch_of(stack_of(depth + 2)), scratch_of(product_of(depth + 2))],
        flops=flops(depth + 2),
    )
    rows_four = exchange(totals)
    taps = pltpu.VMEM((9 * channels, (depth + 2) * cells), bf16)

    length = 8 * pl.cdiv(columns, 8 * devices)
    pieces_shape = sds((devices, length, 2 * channels), bf16)
    pieces = call(
        functools.partial(kernel_grads, cell_count),
        pieces_shape,
        rows_one, rows_four, normed_one, gradient_one, own_stack, near_stack, cotan_two, hidden_stack,
        scratch=[taps, taps, pltpu.VMEM((devices * length, 2 * channels), f32)],
        flops=flops(depth + 2),
    )
    pieces = lax.all_to_all(pieces, AXES, 0, 0)
    sums, squares = call(
        functools.partial(piece_sums, patients),
        (sds((patients, length, 2 * channels), f32), sds((devices, 128), f32)),
        pieces,
    )
    squares = lax.all_to_all(squares, AXES, 0, 0)
    pieces = call(functools.partial(clipped, patients), pieces_shape, squares, sums)
    pieces = lax.all_to_all(pieces, AXES, 0, 0)
    flat = (2 * channels, columns)
    state_next, weights_next = call(
        update,
        (sds(flat, f32), sds(flat, f32)),
        pieces, weights.reshape(flat), prev_state.reshape(flat), tree_noise.reshape(flat),
        scratch=[pltpu.VMEM((devices * length, 2 * channels), f32)],
    )
    return (state_next.reshape(weights.shape), weights_next.reshape(weights.shape))


def solution(mesh):
    return jax.shard_map(
        per_device,
        mesh=mesh,
        in_specs=(P("pat", None, "slab", None), P("pat", None, "slab", None), P(), P(), P()),
        out_specs=(P(), P()),
        check_vma=False,
    )
```

```python
import functools

import jax
import jax.numpy as jnp
from jax import lax
from jax.experimental import pallas as pl
from jax.experimental.pallas import tpu as pltpu
from jax.sharding import PartitionSpec as P


W = 24

eps_norm = 1e-05
clip_bound = 400.0
step_rate = 0.1

f32 = jnp.float32
bf16 = jnp.bfloat16

AXES = ("pat", "slab")
FEATURE_HALO = 3
COTAN_HALO = 1
EARLY = 10**10


def call(kernel, out_shape, *args, scratch=(), flops=0):
    vmem = pl.BlockSpec(memory_space=pltpu.VMEM)
    size = sum(a.size * a.dtype.itemsize for a in args)
    return pl.pallas_call(
        kernel,
        out_shape=out_shape,
        in_specs=[vmem] * len(args),
        out_specs=jax.tree.map(lambda _: vmem, out_shape),
        scratch_shapes=list(scratch),
        cost_estimate=pl.CostEstimate(flops=flops, bytes_accessed=size, transcendentals=0),
        compiler_params=pltpu.CompilerParams(vmem_limit_bytes=18 * 2**20),
    )(*args)


def sds(shape, dtype):
    return jax.ShapeDtypeStruct(shape, dtype)


def patches(plane, stack, z):
    channels, cells = plane.shape
    column = lax.broadcasted_iota(jnp.int32, (1, cells), 1) % W
    span = slice(z * cells, (z + 1) * cells)
    stack[0:channels, span] = pltpu.roll(plane, 1, 1) * (column != 0).astype(bf16)
    stack[channels : 2 * channels, span] = plane
    stack[2 * channels : 3 * channels, span] = pltpu.roll(plane, cells - 1, 1) * (
        column != W - 1
    ).astype(bf16)


def products(planes, kernel, stack, product):
    count = len(planes)

    def fill(z):
        plane = planes[z]() if callable(planes[z]) else planes[z]
        patches(plane, stack, z)
        return plane.shape[1]

    cells = fill(0)
    if count > 1:
        fill(1)
    for z in range(0, count, 2):
        for ahead in range(z + 2, min(z + 4, count)):
            fill(ahead)
        span = slice(z * cells, min(z + 2, count) * cells)
        product[:, span] = jnp.dot(kernel[...], stack[:, span], preferred_element_type=f32)


def tap(product, a, b, z, channels, cells):
    at = 3 * a + b
    return product[at * channels : (at + 1) * channels, z * cells : (z + 1) * cells]


def row_shift(value, rows):
    if rows == 0:
        return value
    cells = value.shape[1]
    cell = lax.broadcasted_iota(jnp.int32, (1, cells), 1)
    kept = cell < cells - W if rows > 0 else cell >= W
    moved = pltpu.roll(value, (-rows * W) % cells, 1)
    if value.dtype == bf16:
        return moved * kept.astype(bf16)
    return jnp.where(kept, moved, 0.0)


def tap_sum(part, z):
    total = None
    for b in range(3):
        rows = part(0, b, z - 1) + part(1, b, z) + part(2, b, z + 1)
        total = add_to(total, row_shift(rows, b - 1))
    return total


def depth_sum(product, z, channels, cells):
    return tap_sum(lambda a, b, at: tap(product, a, b, at + 1, channels, cells), z)


def eye(size):
    return lax.broadcasted_iota(jnp.int32, (size, size), 0) == lax.broadcasted_iota(
        jnp.int32, (size, size), 1
    )


def to_row(first, second):
    both = jnp.concatenate([first, second], axis=0)
    size = both.shape[0]
    return jnp.sum(jnp.where(eye(size), both, 0.0), axis=0, keepdims=True)


def to_columns(rows):
    row = jnp.sum(rows, axis=0, keepdims=True)
    size = row.shape[1]
    both = jnp.sum(jnp.where(eye(size), row, 0.0), axis=1, keepdims=True)
    return both[: size // 2], both[size // 2 :]


def moments(rows, cell_count):
    totals, squares = to_columns(rows)
    centre = totals / cell_count
    return centre, lax.rsqrt(squares / cell_count - centre * centre + eps_norm)


def sigmoid(values):
    return 1.0 / (1.0 + jnp.exp(-values))


def slope(values):
    gate = sigmoid(values)
    return gate * (1.0 + values * (1.0 - gate))


def add_to(total, value):
    return value if total is None else total + value


def send_totals(ref, first, second):
    row = to_row(
        jnp.sum(first, axis=1, keepdims=True), jnp.sum(second, axis=1, keepdims=True)
    )
    ref[...] = jnp.broadcast_to(row, ref.shape)


def inside(z, halo, depth, slab, peers, value):
    if z < halo:
        return jnp.where(slab > 0, value, jnp.zeros_like(value))
    if z >= halo + depth:
        return jnp.where(slab < peers - 1, value, jnp.zeros_like(value))
    return value


def cut_near(own, near_even, near_odd):
    depth = own.shape[0]
    even = lax.axis_index("slab") % 2 == 0
    for near, last in ((near_even, even), (near_odd, ~even)):
        near[0] = own[jnp.where(last, depth - 1, 0)]


def cut_far(own, cotan, far_even, far_odd):
    depth = own.shape[0]
    even = lax.axis_index("slab") % 2 == 0
    for far, last in ((far_even, even), (far_odd, ~even)):
        for z in range(FEATURE_HALO - 1):
            far[z] = own[jnp.where(last, depth - FEATURE_HALO, 1) + z]
        far[FEATURE_HALO - 1] = cotan[jnp.where(last, depth - 1, 0)]


def halo_plane(even_recv, odd_recv, z, before, slab, peers):
    even = slab % 2 == 0
    picked = jnp.where(even == before, odd_recv[z], even_recv[z])
    return jnp.where(slab == (0 if before else peers - 1), jnp.zeros_like(picked), picked)


def kernel_stack(rounded, target):
    channels = rounded.shape[0]
    width = 3 * channels
    for at in range(9):
        target[at * channels : (at + 1) * channels, :] = rounded[:, at * width : (at + 1) * width]


def own_products(weights, own, kernel, kernel_two, back, stack, product):
    channels = weights.shape[1]
    kernel_stack(weights[0].astype(bf16), kernel)
    products([own[z] for z in range(own.shape[0])], kernel, stack, product)
    kernel_stack(weights[1].astype(bf16), kernel_two)
    turned = weights[1].T
    for at in range(9):
        for e in range(3):
            block = (8 - at) * 3 + 2 - e
            back[at * channels : (at + 1) * channels, e * channels : (e + 1) * channels] = turned[
                block * channels : (block + 1) * channels, :
            ].astype(bf16)


def first_conv(peers, near_even, near_odd, kernel, own_product, first, totals, stack, product):
    slab = lax.axis_index("slab")
    depth, channels, cells = first.shape
    planes = [halo_plane(near_even, near_odd, 0, before, slab, peers) for before in (True, False)]
    products(planes, kernel, stack, product)

    def part(a, b, z):
        if 0 <= z < depth:
            return tap(own_product, a, b, z, channels, cells)
        return tap(product, a, b, 0 if z < 0 else 1, channels, cells)

    s = q = None
    for z in range(depth):
        value = tap_sum(part, z)
        first[z] = value
        s, q = add_to(s, value), add_to(q, value * value)
    send_totals(totals, s, q)


def first_conv_edges(peers, far_even, far_odd, kernel, own_product, near_product, stack, product):
    slab = lax.axis_index("slab")
    cells = stack.shape[1] // 4
    channels = own_product.shape[0] // 9
    depth = own_product.shape[1] // cells
    planes = [
        halo_plane(far_even, far_odd, z, before, slab, peers) for before in (True, False) for z in (0, 1)
    ]
    products(planes, kernel, stack, product)
    where = {-3: 0, -2: 1, depth + 1: 2, depth + 2: 3}

    def part(a, b, z):
        if 0 <= z < depth:
            return tap(own_product, a, b, z, channels, cells)
        if z in (-1, depth):
            return tap(near_product, a, b, 0 if z < 0 else 1, channels, cells)
        return tap(product, a, b, where[z], channels, cells)

    return [tap_sum(part, z) for z in (-2, -1, depth, depth + 1)]


def second_conv(
    peers, cell_count, rows, first, far_even, far_odd, kernel_one, own_product, near_product, kernel,
    second, totals, stack, product, far_stack, far_product,
):
    edges = first_conv_edges(
        peers, far_even, far_odd, kernel_one, own_product, near_product, far_stack, far_product
    )
    slab = lax.axis_index("slab")
    depth, channels, cells = first.shape
    centre, spread = moments(rows[...], cell_count)

    def plane(z):
        at = z - 2
        source = first[at] if 0 <= at < depth else edges[z if z < 2 else z - depth]
        normed = (source - centre) * spread
        return inside(z, 2, depth, slab, peers, (normed * sigmoid(normed)).astype(bf16))

    products([functools.partial(plane, z) for z in range(depth + 4)], kernel, stack, product)
    s = q = None
    for z in range(depth + 2):
        value = depth_sum(product, z, channels, cells)
        second[z] = value
        if 1 <= z < depth + 1:
            s, q = add_to(s, value), add_to(q, value * value)
    send_totals(totals, s, q)


def second_gradient(peers, cell_count, rows, second, cotan, far_even, far_odd, gradient, totals):
    slab = lax.axis_index("slab")
    depth = cotan.shape[0]
    centre, spread = moments(rows[...], cell_count)
    s = q = None
    for z in range(depth + 2):
        if 1 <= z < depth + 1:
            upstream = cotan[z - 1]
        else:
            upstream = halo_plane(far_even, far_odd, FEATURE_HALO - 1, z == 0, slab, peers)
        normed = (second[z] - centre) * spread
        value = upstream.astype(f32) * slope(normed)
        gradient[z] = value
        if 1 <= z < depth + 1:
            s, q = add_to(s, value), add_to(q, value * normed)
    send_totals(totals, s, q)


def back_conv(
    peers, cell_count, rows_one, rows_two, rows, first, second, gradient, kernel,
    cotan_two, gradient_one, normed_one, stack, product,
):
    slab = lax.axis_index("slab")
    extended, channels, cells = second.shape
    depth = extended - 2
    centre, spread = moments(rows_two[...], cell_count)
    mean, crossed = (x / cell_count for x in to_columns(rows[...]))

    def plane(z):
        normed = (second[z] - centre) * spread
        value = (spread * (gradient[z] - mean - normed * crossed)).astype(bf16)
        value = inside(z, 1, depth, slab, peers, value)
        if 1 <= z < depth + 1:
            cotan_two[z - 1] = value
        return value

    products([functools.partial(plane, z) for z in range(extended)], kernel, stack, product)
    centre, spread = moments(rows_one[...], cell_count)
    for z in range(depth):
        normed = (first[z] - centre) * spread
        normed_one[z] = normed
        gradient_one[z] = depth_sum(product, z, channels, cells) * slope(normed)


def fill_taps(cotans, taps, at):
    rows, cells = cotans[0].shape
    for z, plane in enumerate(cotans):
        for b in range(3):
            taps[at + b * rows : at + (b + 1) * rows, z * cells : (z + 1) * cells] = row_shift(plane, 1 - b)


def contract(stack, taps, depth, cells):
    windows = [stack[:, a * cells : (a + depth) * cells] for a in range(3)]
    return lax.dot_general(
        jnp.concatenate(windows, axis=0), taps, (((1,), (1,)), ((), ())), preferred_element_type=f32
    )


def extra_rows(length):
    return 8 * pl.cdiv(length + 7, 16)


def three_parts(row):
    parts = []
    for _ in range(3):
        part = row.astype(bf16).astype(f32)
        parts.append(part)
        row = row - part
    return parts


def kernel_grads(
    cell_count, rows_one, normed_one, gradient_one, own_stack, near_stack, cotan_two, hidden_stack,
    pieces, stack, taps_one, taps_two, gathered, side, ones_rows,
):
    depth, channels, cells = normed_one.shape
    count, rows, lanes = pieces.shape
    length = gathered.shape[0] // count
    half = rows - length
    _, spread = moments(rows_one[...], cell_count)
    s = q = None
    for z in range(depth):
        s, q = add_to(s, gradient_one[z]), add_to(q, gradient_one[z] * normed_one[z])
    s = jnp.sum(s, axis=1, keepdims=True)
    q = jnp.sum(q, axis=1, keepdims=True)
    mean, crossed = s / (depth * cells), q / (depth * cells)
    centred, normed = [], []
    for z in range(depth):
        value = spread * (gradient_one[z] - mean - normed_one[z] * crossed)
        centred.append(value.astype(bf16))
        normed.append((spread * normed_one[z]).astype(bf16))
    stack[:, :cells] = near_stack[:, :cells]
    stack[:, cells : (depth + 1) * cells] = own_stack[...]
    stack[:, (depth + 1) * cells :] = near_stack[:, cells:]
    width = 3 * channels
    fill_taps(centred, taps_one, 0)
    fill_taps(normed, taps_one, width)
    cell = lax.broadcasted_iota(jnp.int32, (16, cells), 1)
    tap_row = lax.broadcasted_iota(jnp.int32, (16, cells), 0)
    ones = jnp.where(
        ((tap_row == 0) & (cell < cells - W)) | (tap_row == 1) | ((tap_row == 2) & (cell >= W)), 1.0, 0.0
    ).astype(bf16)
    for z in range(depth):
        taps_one[2 * width :, z * cells : (z + 1) * cells] = ones
    fill_taps([cotan_two[z] for z in range(depth)], taps_two, 0)
    grad_one = contract(stack, taps_one[...], depth, cells)
    grad_two = contract(hidden_stack.at[:, cells : (depth + 3) * cells], taps_two[...], depth, cells)
    for b in range(3):
        at = slice(b * 3 * width, (b + 1) * 3 * width)
        span = slice(b * channels, (b + 1) * channels)
        gathered[at, :channels] = grad_one[:, span]
        gathered[at, channels:] = grad_two[:, span]
        side[at, :channels] = grad_one[:, width + b * channels : width + (b + 1) * channels]
    total = 9 * width
    if count * length > total:
        gathered[total:, :] = jnp.zeros((count * length - total, lanes), f32)
        side[total:, :] = jnp.zeros((count * length - total, lanes), f32)
    turned = grad_one[:, 2 * width :].T
    ones_rows[:, :channels] = jnp.zeros((1, channels), f32)
    for b in range(3):
        start = channels + b * 3 * width
        ones_rows[:, start : start + 3 * width] = turned[b : b + 1, :]
    ones_rows[:, channels + total :] = jnp.zeros((1, ones_rows.shape[1] - channels - total), f32)
    row = to_row(spread * s, q)
    sums = three_parts(row)
    tail = jnp.concatenate(
        [pltpu.roll(part, channels, 1) for part in sums] + sums + [jnp.zeros((1, lanes), f32)], axis=0
    )
    left = lax.broadcasted_iota(jnp.int32, (half, lanes), 1) < channels
    for j in range(count):
        pieces[j, :length] = gathered[j * length : (j + 1) * length, :].astype(bf16)
        first = side[j * length : j * length + half, :]
        further = jnp.concatenate([tail, ones_rows[:, j * length : j * length + lanes]], axis=0)
        if length > half:
            second = pltpu.roll(side[j * length + half : (j + 1) * length, :], channels, 1)
            further = jnp.concatenate([second, further], axis=0)
        if further.shape[0] < half:
            pad = jnp.zeros((half - further.shape[0], lanes), f32)
            further = jnp.concatenate([further, pad], axis=0)
        pieces[j, length:] = jnp.where(left, first, further).astype(bf16)


def piece_sums(patients, cells, pieces, sums, squares):
    count, rows, lanes = pieces.shape
    length = sums.shape[1]
    half, channels = rows - length, lanes // 2
    peers = count // patients
    start = length + max(length - half, 0)
    further = jnp.concatenate([pieces[c, start : start + 8] for c in range(count)], axis=0)
    target = lax.broadcasted_iota(jnp.int32, (3 * count, 8 * count), 0)
    source = lax.broadcasted_iota(jnp.int32, (3 * count, 8 * count), 1)
    offset = source - 8 * (target % count)
    part = target // count
    picked = (offset >= 3 * part) & (offset < 3 * part + 3) & (part < 2) | (part == 2) & (offset == 7)
    picks = jnp.dot(jnp.where(picked, 1.0, 0.0).astype(bf16), further, preferred_element_type=f32)
    lower = lax.broadcasted_iota(jnp.int32, (3 * count, lanes), 1) < channels
    picks = jnp.where(lower, pltpu.roll(picks, channels, 1), 0.0)

    lane = lax.broadcasted_iota(jnp.int32, (1, squares.shape[1]), 1)
    row = jnp.zeros((1, squares.shape[1]), f32)
    for p in range(patients):
        means, crosses, ones = (
            picks[at * count + p * peers : at * count + (p + 1) * peers] for at in range(3)
        )
        means, crosses = (
            jnp.sum(x, axis=0, keepdims=True) / (cells * peers) - x / cells for x in (means, crosses)
        )
        total = -lax.dot_general(
            ones, means, (((0,), (0,)), ((), ())), precision=lax.Precision.HIGHEST, preferred_element_type=f32
        )[:length]
        for j in range(peers):
            piece = pieces.at[p * peers + j]
            normed = piece[length : length + min(length, half)].astype(f32)
            if length > half:
                second = pltpu.roll(piece[length : 2 * length - half].astype(f32), channels, 1)
                normed = jnp.concatenate([normed, second], axis=0)
            total = total + piece[:length].astype(f32) - crosses[j : j + 1] * normed
        sums[p] = total
        part_of = jnp.sum(jnp.sum(total * total, axis=0, keepdims=True), axis=1, keepdims=True)
        row = jnp.where(lane == p, part_of, row)
    squares[...] = jnp.broadcast_to(row, squares.shape)


def clipped(patients, squares, sums, pieces):
    row = jnp.sum(squares[...], axis=0, keepdims=True)
    factor = clip_bound / jnp.maximum(jnp.sqrt(row), clip_bound)
    total = None
    for p in range(patients):
        total = add_to(total, sums[p] * factor[:, p : p + 1])
    rounded = total.astype(bf16)
    for j in range(pieces.shape[0]):
        pieces[j] = rounded


def update(pieces, weights, prev_state, tree_noise, state_next, weights_next, gathered):
    count, length, lanes = pieces.shape
    width = 3 * (lanes // 2)
    for j in range(count):
        gathered[j * length : (j + 1) * length, :] = pieces[j].astype(f32)

    def block(at):
        row = (at % 3 * 3 + at // 3) * width
        return gathered[row : row + width, :]

    for at in range(0, 9, 2):
        group = range(at, min(at + 2, 9))
        span = slice(at * width, (group[-1] + 1) * width)
        combined = jnp.concatenate([block(i) for i in group], axis=0).T
        state_next[:, span] = prev_state[:, span] + combined
        weights_next[:, span] = weights[:, span] - step_rate * (combined + tree_noise[:, span])


def trade(planes, pairs):
    return lax.ppermute(planes, "slab", pairs)


def exchange(rows):
    return lax.all_to_all(rows, "slab", 0, 0)


def per_device(features, cotangent, weights, prev_state, tree_noise):
    peers, patients = lax.axis_size("slab"), lax.axis_size("pat")
    devices = peers * patients
    own = features[0].transpose(1, 0, 2)
    cotan = cotangent[0].transpose(1, 0, 2)
    depth, channels, cells = own.shape
    cell_count = peers * depth * cells
    columns = weights.shape[2]
    rows_shape = sds((peers, 2 * channels), f32)

    def field(planes, dtype):
        return sds((planes, channels, cells), dtype)

    def stack_of(planes):
        return sds((3 * channels, planes * cells), bf16)

    def product_of(planes):
        return sds((9 * channels, planes * cells), f32)

    def scratch_of(shape):
        return pltpu.VMEM(shape.shape, shape.dtype)

    def flops(planes):
        return 2 * 27 * channels * channels * cells * planes

    far = field(FEATURE_HALO - 1 + COTAN_HALO, bf16)
    near_even, near_odd = call(cut_near, (field(1, bf16),) * 2, own, flops=EARLY)
    far_even, far_odd = call(cut_far, (far,) * 2, own, cotan)
    even_pairs = [(i, i ^ 1) for i in range(peers)]
    odd_pairs = [(i, (i + 1) % peers if i % 2 else (i - 1) % peers) for i in range(peers)]
    near_even = trade(near_even, even_pairs)
    near_odd = trade(near_odd, odd_pairs)
    far_even = trade(far_even, even_pairs)
    far_odd = trade(far_odd, odd_pairs)

    kernel_shape = sds((9 * channels, 3 * channels), bf16)
    kernel_one, kernel_two, kernel_back, own_stack, own_product = call(
        own_products,
        (kernel_shape, kernel_shape, kernel_shape, stack_of(depth), product_of(depth)),
        weights, own,
        flops=flops(depth),
    )
    first, totals, near_stack, near_product = call(
        functools.partial(first_conv, peers),
        (field(depth, f32), rows_shape, stack_of(2), product_of(2)),
        near_even, near_odd, kernel_one, own_product,
        flops=flops(2),
    )
    rows_one = exchange(totals)
    second, totals, hidden_stack = call(
        functools.partial(second_conv, peers, cell_count),
        (field(depth + 2, f32), rows_shape, stack_of(depth + 4)),
        rows_one, first, far_even, far_odd, kernel_one, own_product, near_product, kernel_two,
        scratch=[scratch_of(product_of(depth + 4)), scratch_of(stack_of(4)), scratch_of(product_of(4))],
        flops=flops(depth + 4),
    )
    rows_two = exchange(totals)
    gradient_two, totals = call(
        functools.partial(second_gradient, peers, cell_count),
        (field(depth + 2, f32), rows_shape),
        rows_two, second, cotan, far_even, far_odd,
    )
    rows_three = exchange(totals)
    cotan_two, gradient_one, normed_one = call(
        functools.partial(back_conv, peers, cell_count),
        (field(depth, bf16), field(depth, f32), field(depth, f32)),
        rows_one, rows_two, rows_three, first, second, gradient_two, kernel_back,
        scratch=[scratch_of(stack_of(depth + 2)), scratch_of(product_of(depth + 2))],
        flops=flops(depth + 2),
    )

    length = 8 * pl.cdiv(columns, 8 * devices)
    taps = pltpu.VMEM((3 * channels, depth * cells), bf16)
    pieces = call(
        functools.partial(kernel_grads, cell_count),
        sds((devices, length + extra_rows(length), 2 * channels), bf16),
        rows_one, normed_one, gradient_one, own_stack, near_stack, cotan_two, hidden_stack,
        scratch=[
            scratch_of(stack_of(depth + 2)),
            pltpu.VMEM((6 * channels + 16, depth * cells), bf16),
            taps,
            pltpu.VMEM((devices * length, 2 * channels), f32),
            pltpu.VMEM((devices * length, 2 * channels), f32),
            pltpu.VMEM((1, devices * length + 4 * channels), f32),
        ],
        flops=3 * flops(depth),
    )
    pieces = lax.all_to_all(pieces, AXES, 0, 0)
    sums, squares = call(
        functools.partial(piece_sums, patients, depth * cells),
        (sds((patients, length, 2 * channels), f32), sds((devices, 128), f32)),
        pieces,
    )
    pieces_shape = sds((peers, length, 2 * channels), bf16)
    squares = lax.all_to_all(squares, AXES, 0, 0)
    pieces = call(functools.partial(clipped, patients), pieces_shape, squares, sums)
    pieces = lax.all_gather(lax.all_to_all(pieces, "slab", 0, 0), "pat", tiled=True)
    flat = (2 * channels, columns)
    state_next, weights_next = call(
        update,
        (sds(flat, f32), sds(flat, f32)),
        pieces, weights.reshape(flat), prev_state.reshape(flat), tree_noise.reshape(flat),
        scratch=[pltpu.VMEM((devices * length, 2 * channels), f32)],
    )
    return (state_next.reshape(weights.shape), weights_next.reshape(weights.shape))


def solution(mesh):
    return jax.shard_map(
        per_device,
        mesh=mesh,
        in_specs=(P("pat", None, "slab", None), P("pat", None, "slab", None), P(), P(), P()),
        out_specs=(P(), P()),
        check_vma=False,
    )
```

```python
import functools

import jax
import jax.numpy as jnp
from jax import lax
from jax.experimental import pallas as pl
from jax.experimental.pallas import tpu as pltpu
from jax.sharding import PartitionSpec as P


W = 24

eps_norm = 1e-05
clip_bound = 400.0
step_rate = 0.1

f32 = jnp.float32
bf16 = jnp.bfloat16

AXES = ("pat", "slab")
FEATURE_HALO = 3
COTAN_HALO = 1
EARLY = 10**10


def call(kernel, out_shape, *args, scratch=(), flops=0):
    vmem = pl.BlockSpec(memory_space=pltpu.VMEM)
    size = sum(a.size * a.dtype.itemsize for a in args)
    return pl.pallas_call(
        kernel,
        out_shape=out_shape,
        in_specs=[vmem] * len(args),
        out_specs=jax.tree.map(lambda _: vmem, out_shape),
        scratch_shapes=list(scratch),
        cost_estimate=pl.CostEstimate(flops=flops, bytes_accessed=size, transcendentals=0),
        compiler_params=pltpu.CompilerParams(vmem_limit_bytes=18 * 2**20),
    )(*args)


def sds(shape, dtype):
    return jax.ShapeDtypeStruct(shape, dtype)


def patches(plane, stack, z):
    channels, cells = plane.shape
    column = lax.broadcasted_iota(jnp.int32, (1, cells), 1) % W
    span = slice(z * cells, (z + 1) * cells)
    stack[0:channels, span] = pltpu.roll(plane, 1, 1) * (column != 0).astype(bf16)
    stack[channels : 2 * channels, span] = plane
    stack[2 * channels : 3 * channels, span] = pltpu.roll(plane, cells - 1, 1) * (
        column != W - 1
    ).astype(bf16)


def products(planes, kernel, stack, product, trimmed=False):
    count = len(planes)
    trimmed = trimmed and count % 2 == 0
    third = kernel.shape[0] // 3

    def fill(z):
        plane = planes[z]() if callable(planes[z]) else planes[z]
        patches(plane, stack, z)
        return plane.shape[1]

    cells = fill(0)
    if count > 1:
        fill(1)
    for z in range(0, count, 2):
        for ahead in range(z + 2, min(z + 4, count)):
            fill(ahead)
        span = slice(z * cells, min(z + 2, count) * cells)
        work = [(slice(None), span)]
        if trimmed and z == 0:
            work = [(slice(third), span), (slice(third, 2 * third), slice(cells, 2 * cells))]
        elif trimmed and z == count - 2:
            work = [(slice(2 * third, None), span), (slice(third, 2 * third), slice(z * cells, (z + 1) * cells))]
        for rows, columns in work:
            product[rows, columns] = jnp.dot(kernel[rows, :], stack[:, columns], preferred_element_type=f32)


def tap(product, a, b, z, channels, cells):
    at = 3 * a + b
    return product[at * channels : (at + 1) * channels, z * cells : (z + 1) * cells]


def row_shift(value, rows):
    if rows == 0:
        return value
    cells = value.shape[1]
    cell = lax.broadcasted_iota(jnp.int32, (1, cells), 1)
    kept = cell < cells - W if rows > 0 else cell >= W
    moved = pltpu.roll(value, (-rows * W) % cells, 1)
    if value.dtype == bf16:
        return moved * kept.astype(bf16)
    return jnp.where(kept, moved, 0.0)


def tap_sum(part, z):
    total = None
    for b in range(3):
        rows = part(0, b, z - 1) + part(1, b, z) + part(2, b, z + 1)
        total = add_to(total, row_shift(rows, b - 1))
    return total


def depth_sum(product, z, channels, cells):
    return tap_sum(lambda a, b, at: tap(product, a, b, at + 1, channels, cells), z)


def eye(size):
    return lax.broadcasted_iota(jnp.int32, (size, size), 0) == lax.broadcasted_iota(
        jnp.int32, (size, size), 1
    )


def to_row(first, second):
    both = jnp.concatenate([first, second], axis=0)
    size = both.shape[0]
    return jnp.sum(jnp.where(eye(size), both, 0.0), axis=0, keepdims=True)


def to_columns(rows):
    row = jnp.sum(rows, axis=0, keepdims=True)
    size = row.shape[1]
    both = jnp.sum(jnp.where(eye(size), row, 0.0), axis=1, keepdims=True)
    return both[: size // 2], both[size // 2 :]


def moments(rows, cell_count):
    totals, squares = to_columns(rows)
    centre = totals / cell_count
    return centre, lax.rsqrt(squares / cell_count - centre * centre + eps_norm)


def sigmoid(values):
    return 1.0 / (1.0 + jnp.exp(-values))


def slope(values):
    gate = sigmoid(values)
    return gate * (1.0 + values * (1.0 - gate))


def add_to(total, value):
    return value if total is None else total + value


def send_totals(ref, first, second):
    row = to_row(
        jnp.sum(first, axis=1, keepdims=True), jnp.sum(second, axis=1, keepdims=True)
    )
    ref[...] = jnp.broadcast_to(row, ref.shape)


def inside(z, halo, depth, slab, peers, value):
    if z < halo:
        return jnp.where(slab > 0, value, jnp.zeros_like(value))
    if z >= halo + depth:
        return jnp.where(slab < peers - 1, value, jnp.zeros_like(value))
    return value


def cut_near(own, near_even, near_odd):
    depth = own.shape[0]
    even = lax.axis_index("slab") % 2 == 0
    for near, last in ((near_even, even), (near_odd, ~even)):
        near[0] = own[jnp.where(last, depth - 1, 0)]


def cut_far(own, cotan, far_even, far_odd):
    depth = own.shape[0]
    even = lax.axis_index("slab") % 2 == 0
    for far, last in ((far_even, even), (far_odd, ~even)):
        for z in range(FEATURE_HALO - 1):
            far[z] = own[jnp.where(last, depth - FEATURE_HALO, 1) + z]
        far[FEATURE_HALO - 1] = cotan[jnp.where(last, depth - 1, 0)]


def halo_plane(even_recv, odd_recv, z, before, slab, peers):
    even = slab % 2 == 0
    picked = jnp.where(even == before, odd_recv[z], even_recv[z])
    return jnp.where(slab == (0 if before else peers - 1), jnp.zeros_like(picked), picked)


def kernel_stack(rounded, target):
    channels = rounded.shape[0]
    width = 3 * channels
    for at in range(9):
        target[at * channels : (at + 1) * channels, :] = rounded[:, at * width : (at + 1) * width]


def own_products(weights, own, kernel, kernel_two, back, stack, product):
    channels = weights.shape[1]
    kernel_stack(weights[0].astype(bf16), kernel)
    products([own[z] for z in range(own.shape[0])], kernel, stack, product)
    kernel_stack(weights[1].astype(bf16), kernel_two)
    turned = weights[1].T
    for at in range(9):
        for e in range(3):
            block = (8 - at) * 3 + 2 - e
            back[at * channels : (at + 1) * channels, e * channels : (e + 1) * channels] = turned[
                block * channels : (block + 1) * channels, :
            ].astype(bf16)


def first_conv(peers, near_even, near_odd, kernel, own_product, first, totals, stack, product):
    slab = lax.axis_index("slab")
    depth, channels, cells = first.shape
    planes = [halo_plane(near_even, near_odd, 0, before, slab, peers) for before in (True, False)]
    products(planes, kernel, stack, product)

    def part(a, b, z):
        if 0 <= z < depth:
            return tap(own_product, a, b, z, channels, cells)
        return tap(product, a, b, 0 if z < 0 else 1, channels, cells)

    s = q = None
    for z in range(depth):
        value = tap_sum(part, z)
        first[z] = value
        s, q = add_to(s, value), add_to(q, value * value)
    send_totals(totals, s, q)


def first_conv_edges(peers, far_even, far_odd, kernel, own_product, near_product, stack, product):
    slab = lax.axis_index("slab")
    cells = stack.shape[1] // 4
    channels = own_product.shape[0] // 9
    depth = own_product.shape[1] // cells
    planes = [
        halo_plane(far_even, far_odd, z, before, slab, peers) for before in (True, False) for z in (0, 1)
    ]
    products(planes, kernel, stack, product, trimmed=True)
    where = {-3: 0, -2: 1, depth + 1: 2, depth + 2: 3}

    def part(a, b, z):
        if 0 <= z < depth:
            return tap(own_product, a, b, z, channels, cells)
        if z in (-1, depth):
            return tap(near_product, a, b, 0 if z < 0 else 1, channels, cells)
        return tap(product, a, b, where[z], channels, cells)

    return [tap_sum(part, z) for z in (-2, -1, depth, depth + 1)]


def second_conv(
    peers, cell_count, rows, first, far_even, far_odd, kernel_one, own_product, near_product, kernel,
    second, totals, stack, product, far_stack, far_product,
):
    edges = first_conv_edges(
        peers, far_even, far_odd, kernel_one, own_product, near_product, far_stack, far_product
    )
    slab = lax.axis_index("slab")
    depth, channels, cells = first.shape
    centre, spread = moments(rows[...], cell_count)

    def plane(z):
        at = z - 2
        source = first[at] if 0 <= at < depth else edges[z if z < 2 else z - depth]
        normed = (source - centre) * spread
        return inside(z, 2, depth, slab, peers, (normed * sigmoid(normed)).astype(bf16))

    products([functools.partial(plane, z) for z in range(depth + 4)], kernel, stack, product, True)
    s = q = None
    for z in range(depth + 2):
        value = depth_sum(product, z, channels, cells)
        second[z] = value
        if 1 <= z < depth + 1:
            s, q = add_to(s, value), add_to(q, value * value)
    send_totals(totals, s, q)


def second_gradient(peers, cell_count, rows, second, cotan, far_even, far_odd, gradient, totals):
    slab = lax.axis_index("slab")
    depth = cotan.shape[0]
    centre, spread = moments(rows[...], cell_count)
    s = q = None
    for z in range(depth + 2):
        if 1 <= z < depth + 1:
            upstream = cotan[z - 1]
        else:
            upstream = halo_plane(far_even, far_odd, FEATURE_HALO - 1, z == 0, slab, peers)
        normed = (second[z] - centre) * spread
        value = upstream.astype(f32) * slope(normed)
        gradient[z] = value
        if 1 <= z < depth + 1:
            s, q = add_to(s, value), add_to(q, value * normed)
    send_totals(totals, s, q)


def back_conv(
    peers, cell_count, rows_one, rows_two, rows, first, second, gradient, kernel,
    cotan_two, gradient_one, normed_one, stack, product,
):
    slab = lax.axis_index("slab")
    extended, channels, cells = second.shape
    depth = extended - 2
    centre, spread = moments(rows_two[...], cell_count)
    mean, crossed = (x / cell_count for x in to_columns(rows[...]))

    def plane(z):
        normed = (second[z] - centre) * spread
        value = (spread * (gradient[z] - mean - normed * crossed)).astype(bf16)
        value = inside(z, 1, depth, slab, peers, value)
        if 1 <= z < depth + 1:
            cotan_two[z - 1] = value
        return value

    products([functools.partial(plane, z) for z in range(extended)], kernel, stack, product, True)
    centre, spread = moments(rows_one[...], cell_count)
    for z in range(depth):
        normed = (first[z] - centre) * spread
        normed_one[z] = normed
        gradient_one[z] = depth_sum(product, z, channels, cells) * slope(normed)


def fill_taps(cotans, taps, at):
    rows, cells = cotans[0].shape
    for z, plane in enumerate(cotans):
        for b in range(3):
            taps[at + b * rows : at + (b + 1) * rows, z * cells : (z + 1) * cells] = row_shift(plane, 1 - b)


def contract(stack, taps, depth, cells):
    windows = [stack[:, a * cells : (a + depth) * cells] for a in range(3)]
    return lax.dot_general(
        jnp.concatenate(windows, axis=0), taps, (((1,), (1,)), ((), ())), preferred_element_type=f32
    )


def extra_rows(length):
    return 8 * pl.cdiv(length + 7, 16)


def parts_of(row, count):
    parts = []
    for _ in range(count):
        part = row.astype(bf16).astype(f32)
        parts.append(part)
        row = row - part
    return parts


def kernel_grads(
    cell_count, rows_one, normed_one, gradient_one, own_stack, near_stack, cotan_two, hidden_stack,
    pieces, stack, taps_one, taps_two, gathered, side, ones_rows,
):
    depth, channels, cells = normed_one.shape
    count, rows, lanes = pieces.shape
    length = gathered.shape[0] // count
    half = rows - length
    _, spread = moments(rows_one[...], cell_count)
    s = q = m = v = None
    for z in range(depth):
        grad, norm = gradient_one[z], normed_one[z]
        s, q = add_to(s, grad), add_to(q, grad * norm)
        m, v = add_to(m, norm), add_to(v, norm * norm)
    s, q, m, v = (jnp.sum(x, axis=1, keepdims=True) for x in (s, q, m, v))
    size = depth * cells
    tilt = (q / size - s / size * (m / size)) / (v / size - m / size * (m / size) + 1.0)
    tilt = tilt.astype(bf16).astype(f32)
    level = (spread * (s / size - tilt * (m / size))).astype(bf16).astype(f32)
    centred, normed = [], []
    for z in range(depth):
        value = spread * (gradient_one[z] - normed_one[z] * tilt) - level
        centred.append(value.astype(bf16))
        normed.append((spread * normed_one[z]).astype(bf16))
    stack[:, :cells] = near_stack[:, :cells]
    stack[:, cells : (depth + 1) * cells] = own_stack[...]
    stack[:, (depth + 1) * cells :] = near_stack[:, cells:]
    width = 3 * channels
    fill_taps(centred, taps_one, 0)
    fill_taps(normed, taps_one, width)
    cell = lax.broadcasted_iota(jnp.int32, (16, cells), 1)
    tap_row = lax.broadcasted_iota(jnp.int32, (16, cells), 0)
    ones = jnp.where(
        ((tap_row == 0) & (cell < cells - W)) | (tap_row == 1) | ((tap_row == 2) & (cell >= W)), 1.0, 0.0
    ).astype(bf16)
    for z in range(depth):
        taps_one[2 * width :, z * cells : (z + 1) * cells] = ones
    fill_taps([cotan_two[z] for z in range(depth)], taps_two, 0)
    grad_one = contract(stack, taps_one[...], depth, cells)
    grad_two = contract(hidden_stack.at[:, cells : (depth + 3) * cells], taps_two[...], depth, cells)
    for b in range(3):
        at = slice(b * 3 * width, (b + 1) * 3 * width)
        span = slice(b * channels, (b + 1) * channels)
        gathered[at, :channels] = grad_one[:, span]
        gathered[at, channels:] = grad_two[:, span]
        side[at, :channels] = grad_one[:, width + b * channels : width + (b + 1) * channels]
    total = 9 * width
    if count * length > total:
        gathered[total:, :] = jnp.zeros((count * length - total, lanes), f32)
        side[total:, :] = jnp.zeros((count * length - total, lanes), f32)
    turned = grad_one[:, 2 * width :].T
    ones_rows[:, :channels] = jnp.zeros((1, channels), f32)
    for b in range(3):
        start = channels + b * 3 * width
        ones_rows[:, start : start + 3 * width] = turned[b : b + 1, :]
    ones_rows[:, channels + total :] = jnp.zeros((1, ones_rows.shape[1] - channels - total), f32)
    totals, fit = to_row(spread * s, q), to_row(level, tilt)
    tail = jnp.concatenate(
        [pltpu.roll(part, channels, 1) for part in parts_of(totals, 3)]
        + parts_of(totals, 2)
        + [pltpu.roll(fit, channels, 1), fit],
        axis=0,
    )
    left = lax.broadcasted_iota(jnp.int32, (half, lanes), 1) < channels
    for j in range(count):
        pieces[j, :length] = gathered[j * length : (j + 1) * length, :].astype(bf16)
        first = side[j * length : j * length + half, :]
        further = jnp.concatenate([tail, ones_rows[:, j * length : j * length + lanes]], axis=0)
        if length > half:
            second = pltpu.roll(side[j * length + half : (j + 1) * length, :], channels, 1)
            further = jnp.concatenate([second, further], axis=0)
        if further.shape[0] < half:
            pad = jnp.zeros((half - further.shape[0], lanes), f32)
            further = jnp.concatenate([further, pad], axis=0)
        pieces[j, length:] = jnp.where(left, first, further).astype(bf16)


def piece_sums(patients, cells, pieces, sums, squares):
    count, rows, lanes = pieces.shape
    length = sums.shape[1]
    half, channels = rows - length, lanes // 2
    peers = count // patients
    start = length + max(length - half, 0)
    further = jnp.concatenate([pieces[c, start : start + 8] for c in range(count)], axis=0)
    starts = (0, 3, 5, 6, 7, 8)
    kinds = len(starts) - 1
    target = lax.broadcasted_iota(jnp.int32, (kinds * count, 8 * count), 0)
    offset = lax.broadcasted_iota(jnp.int32, (kinds * count, 8 * count), 1) - 8 * (target % count)
    picked = offset < 0
    for at in range(kinds):
        picked |= (target // count == at) & (offset >= starts[at]) & (offset < starts[at + 1])
    picked &= offset >= 0
    picks = jnp.dot(jnp.where(picked, 1.0, 0.0).astype(bf16), further, preferred_element_type=f32)
    lower = lax.broadcasted_iota(jnp.int32, (kinds * count, lanes), 1) < channels
    picks = jnp.where(lower, pltpu.roll(picks, channels, 1), 0.0)

    lane = lax.broadcasted_iota(jnp.int32, (1, squares.shape[1]), 1)
    row = jnp.zeros((1, squares.shape[1]), f32)
    for p in range(patients):
        means, crosses, levels, tilts, ones = (
            picks[at * count + p * peers : at * count + (p + 1) * peers] for at in range(kinds)
        )
        means = jnp.sum(means, axis=0, keepdims=True) / (cells * peers) - levels
        crosses = jnp.sum(crosses, axis=0, keepdims=True) / (cells * peers) - tilts
        total = -lax.dot_general(
            ones, means, (((0,), (0,)), ((), ())), precision=lax.Precision.HIGHEST, preferred_element_type=f32
        )[:length]
        for j in range(peers):
            piece = pieces.at[p * peers + j]
            normed = piece[length : length + min(length, half)].astype(f32)
            if length > half:
                second = pltpu.roll(piece[length : 2 * length - half].astype(f32), channels, 1)
                normed = jnp.concatenate([normed, second], axis=0)
            total = total + piece[:length].astype(f32) - crosses[j : j + 1] * normed
        sums[p] = total
        part_of = jnp.sum(jnp.sum(total * total, axis=0, keepdims=True), axis=1, keepdims=True)
        row = jnp.where(lane == p, part_of, row)
    squares[...] = jnp.broadcast_to(row, squares.shape)


def clipped(patients, squares, sums, pieces):
    row = jnp.sum(squares[...], axis=0, keepdims=True)
    factor = clip_bound / jnp.maximum(jnp.sqrt(row), clip_bound)
    total = None
    for p in range(patients):
        total = add_to(total, sums[p] * factor[:, p : p + 1])
    rounded = total.astype(bf16)
    for j in range(pieces.shape[0]):
        pieces[j] = rounded


def update(pieces, weights, prev_state, tree_noise, state_next, weights_next, gathered):
    count, length, lanes = pieces.shape
    width = 3 * (lanes // 2)
    for j in range(count):
        gathered[j * length : (j + 1) * length, :] = pieces[j].astype(f32)

    def block(at):
        row = (at % 3 * 3 + at // 3) * width
        return gathered[row : row + width, :]

    for at in range(0, 9, 2):
        group = range(at, min(at + 2, 9))
        span = slice(at * width, (group[-1] + 1) * width)
        combined = jnp.concatenate([block(i) for i in group], axis=0).T
        state_next[:, span] = prev_state[:, span] + combined
        weights_next[:, span] = weights[:, span] - step_rate * (combined + tree_noise[:, span])


def trade(planes, pairs):
    return lax.ppermute(planes, "slab", pairs)


def exchange(rows):
    return lax.all_to_all(rows, "slab", 0, 0)


def per_device(features, cotangent, weights, prev_state, tree_noise):
    peers, patients = lax.axis_size("slab"), lax.axis_size("pat")
    devices = peers * patients
    own = features[0].transpose(1, 0, 2)
    cotan = cotangent[0].transpose(1, 0, 2)
    depth, channels, cells = own.shape
    cell_count = peers * depth * cells
    columns = weights.shape[2]
    rows_shape = sds((peers, 2 * channels), f32)

    def field(planes, dtype):
        return sds((planes, channels, cells), dtype)

    def stack_of(planes):
        return sds((3 * channels, planes * cells), bf16)

    def product_of(planes):
        return sds((9 * channels, planes * cells), f32)

    def scratch_of(shape):
        return pltpu.VMEM(shape.shape, shape.dtype)

    def flops(planes):
        return 2 * 27 * channels * channels * cells * planes

    far = field(FEATURE_HALO - 1 + COTAN_HALO, bf16)
    near_even, near_odd = call(cut_near, (field(1, bf16),) * 2, own, flops=EARLY)
    far_even, far_odd = call(cut_far, (far,) * 2, own, cotan)
    even_pairs = [(i, i ^ 1) for i in range(peers)]
    odd_pairs = [(i, (i + 1) % peers if i % 2 else (i - 1) % peers) for i in range(peers)]
    near_even = trade(near_even, even_pairs)
    near_odd = trade(near_odd, odd_pairs)
    far_even = trade(far_even, even_pairs)
    far_odd = trade(far_odd, odd_pairs)

    kernel_shape = sds((9 * channels, 3 * channels), bf16)
    kernel_one, kernel_two, kernel_back, own_stack, own_product = call(
        own_products,
        (kernel_shape, kernel_shape, kernel_shape, stack_of(depth), product_of(depth)),
        weights, own,
        flops=flops(depth),
    )
    first, totals, near_stack, near_product = call(
        functools.partial(first_conv, peers),
        (field(depth, f32), rows_shape, stack_of(2), product_of(2)),
        near_even, near_odd, kernel_one, own_product,
        flops=flops(2),
    )
    rows_one = exchange(totals)
    second, totals, hidden_stack = call(
        functools.partial(second_conv, peers, cell_count),
        (field(depth + 2, f32), rows_shape, stack_of(depth + 4)),
        rows_one, first, far_even, far_odd, kernel_one, own_product, near_product, kernel_two,
        scratch=[scratch_of(product_of(depth + 4)), scratch_of(stack_of(4)), scratch_of(product_of(4))],
        flops=flops(depth + 4),
    )
    rows_two = exchange(totals)
    gradient_two, totals = call(
        functools.partial(second_gradient, peers, cell_count),
        (field(depth + 2, f32), rows_shape),
        rows_two, second, cotan, far_even, far_odd,
    )
    rows_three = exchange(totals)
    cotan_two, gradient_one, normed_one = call(
        functools.partial(back_conv, peers, cell_count),
        (field(depth, bf16), field(depth, f32), field(depth, f32)),
        rows_one, rows_two, rows_three, first, second, gradient_two, kernel_back,
        scratch=[scratch_of(stack_of(depth + 2)), scratch_of(product_of(depth + 2))],
        flops=flops(depth + 2),
    )

    length = 8 * pl.cdiv(columns, 8 * devices)
    taps = pltpu.VMEM((3 * channels, depth * cells), bf16)
    pieces = call(
        functools.partial(kernel_grads, cell_count),
        sds((devices, length + extra_rows(length), 2 * channels), bf16),
        rows_one, normed_one, gradient_one, own_stack, near_stack, cotan_two, hidden_stack,
        scratch=[
            scratch_of(stack_of(depth + 2)),
            pltpu.VMEM((6 * channels + 16, depth * cells), bf16),
            taps,
            pltpu.VMEM((devices * length, 2 * channels), f32),
            pltpu.VMEM((devices * length, 2 * channels), f32),
            pltpu.VMEM((1, devices * length + 4 * channels), f32),
        ],
        flops=3 * flops(depth),
    )
    pieces = lax.all_to_all(pieces, AXES, 0, 0)
    sums, squares = call(
        functools.partial(piece_sums, patients, depth * cells),
        (sds((patients, length, 2 * channels), f32), sds((devices, 128), f32)),
        pieces,
    )
    pieces_shape = sds((peers, length, 2 * channels), bf16)
    squares = lax.all_to_all(squares, AXES, 0, 0)
    pieces = call(functools.partial(clipped, patients), pieces_shape, squares, sums)
    pieces = lax.all_gather(lax.all_to_all(pieces, "slab", 0, 0), "pat", tiled=True)
    flat = (2 * channels, columns)
    state_next, weights_next = call(
        update,
        (sds(flat, f32), sds(flat, f32)),
        pieces, weights.reshape(flat), prev_state.reshape(flat), tree_noise.reshape(flat),
        scratch=[pltpu.VMEM((devices * length, 2 * channels), f32)],
    )
    return (state_next.reshape(weights.shape), weights_next.reshape(weights.shape))


def solution(mesh):
    return jax.shard_map(
        per_device,
        mesh=mesh,
        in_specs=(P("pat", None, "slab", None), P("pat", None, "slab", None), P(), P(), P()),
        out_specs=(P(), P()),
        check_vma=False,
    )
```

```python
import functools

import jax
import jax.numpy as jnp
from jax import lax
from jax.experimental import pallas as pl
from jax.experimental.pallas import tpu as pltpu
from jax.sharding import PartitionSpec as P


W = 24

eps_norm = 1e-05
clip_bound = 400.0
step_rate = 0.1

f32 = jnp.float32
bf16 = jnp.bfloat16

AXES = ("pat", "slab")
FEATURE_HALO = 3
COTAN_HALO = 1
EARLY = 10**10


def call(kernel, out_shape, *args, scratch=(), flops=0):
    vmem = pl.BlockSpec(memory_space=pltpu.VMEM)
    size = sum(a.size * a.dtype.itemsize for a in args)
    return pl.pallas_call(
        kernel,
        out_shape=out_shape,
        in_specs=[vmem] * len(args),
        out_specs=jax.tree.map(lambda _: vmem, out_shape),
        scratch_shapes=list(scratch),
        cost_estimate=pl.CostEstimate(flops=flops, bytes_accessed=size, transcendentals=0),
        compiler_params=pltpu.CompilerParams(vmem_limit_bytes=18 * 2**20),
    )(*args)


def sds(shape, dtype):
    return jax.ShapeDtypeStruct(shape, dtype)


def patches(plane, stack, z):
    channels, cells = plane.shape
    column = lax.broadcasted_iota(jnp.int32, (1, cells), 1) % W
    span = slice(z * cells, (z + 1) * cells)
    stack[0:channels, span] = pltpu.roll(plane, 1, 1) * (column != 0).astype(bf16)
    stack[channels : 2 * channels, span] = plane
    stack[2 * channels : 3 * channels, span] = pltpu.roll(plane, cells - 1, 1) * (
        column != W - 1
    ).astype(bf16)


def products(planes, kernel, stack, product, trimmed=False):
    count = len(planes)
    trimmed = trimmed and count % 2 == 0
    third = kernel.shape[0] // 3

    def fill(z):
        plane = planes[z]() if callable(planes[z]) else planes[z]
        patches(plane, stack, z)
        return plane.shape[1]

    cells = fill(0)
    if count > 1:
        fill(1)
    for z in range(0, count, 2):
        for ahead in range(z + 2, min(z + 4, count)):
            fill(ahead)
        span = slice(z * cells, min(z + 2, count) * cells)
        work = [(slice(None), span)]
        if trimmed and z == 0:
            work = [(slice(third), span), (slice(third, 2 * third), slice(cells, 2 * cells))]
        elif trimmed and z == count - 2:
            work = [(slice(2 * third, None), span), (slice(third, 2 * third), slice(z * cells, (z + 1) * cells))]
        for rows, columns in work:
            product[rows, columns] = jnp.dot(kernel[rows, :], stack[:, columns], preferred_element_type=f32)


def tap(product, a, b, z, channels, cells):
    at = 3 * a + b
    return product[at * channels : (at + 1) * channels, z * cells : (z + 1) * cells]


def row_shift(value, rows):
    if rows == 0:
        return value
    cells = value.shape[1]
    cell = lax.broadcasted_iota(jnp.int32, (1, cells), 1)
    kept = cell < cells - W if rows > 0 else cell >= W
    moved = pltpu.roll(value, (-rows * W) % cells, 1)
    if value.dtype == bf16:
        return moved * kept.astype(bf16)
    return jnp.where(kept, moved, 0.0)


def tap_sum(part, z):
    total = None
    for b in range(3):
        rows = part(0, b, z - 1) + part(1, b, z) + part(2, b, z + 1)
        total = add_to(total, row_shift(rows, b - 1))
    return total


def depth_sum(product, z, channels, cells):
    return tap_sum(lambda a, b, at: tap(product, a, b, at + 1, channels, cells), z)


def eye(size):
    return lax.broadcasted_iota(jnp.int32, (size, size), 0) == lax.broadcasted_iota(
        jnp.int32, (size, size), 1
    )


def to_row(first, second):
    both = jnp.concatenate([first, second], axis=0)
    size = both.shape[0]
    return jnp.sum(jnp.where(eye(size), both, 0.0), axis=0, keepdims=True)


def to_columns(rows):
    row = jnp.sum(rows, axis=0, keepdims=True)
    size = row.shape[1]
    both = jnp.sum(jnp.where(eye(size), row, 0.0), axis=1, keepdims=True)
    return both[: size // 2], both[size // 2 :]


def moments(rows, cell_count):
    totals, squares = to_columns(rows)
    centre = totals / cell_count
    return centre, lax.rsqrt(squares / cell_count - centre * centre + eps_norm)


def sigmoid(values):
    return 1.0 / (1.0 + jnp.exp(-values))


def slope(values):
    gate = sigmoid(values)
    return gate * (1.0 + values * (1.0 - gate))


def add_to(total, value):
    return value if total is None else total + value


def send_totals(ref, first, second):
    row = to_row(
        jnp.sum(first, axis=1, keepdims=True), jnp.sum(second, axis=1, keepdims=True)
    )
    ref[...] = jnp.broadcast_to(row, ref.shape)


def inside(z, halo, depth, slab, peers, value):
    if z < halo:
        return jnp.where(slab > 0, value, jnp.zeros_like(value))
    if z >= halo + depth:
        return jnp.where(slab < peers - 1, value, jnp.zeros_like(value))
    return value


def cut_near(own, near_even, near_odd):
    depth = own.shape[0]
    even = lax.axis_index("slab") % 2 == 0
    for near, last in ((near_even, even), (near_odd, ~even)):
        near[0] = own[jnp.where(last, depth - 1, 0)]


def cut_far(own, cotan, far_even, far_odd):
    depth = own.shape[0]
    even = lax.axis_index("slab") % 2 == 0
    for far, last in ((far_even, even), (far_odd, ~even)):
        for z in range(FEATURE_HALO - 1):
            far[z] = own[jnp.where(last, depth - FEATURE_HALO, 1) + z]
        far[FEATURE_HALO - 1] = cotan[jnp.where(last, depth - 1, 0)]


def halo_plane(even_recv, odd_recv, z, before, slab, peers):
    even = slab % 2 == 0
    picked = jnp.where(even == before, odd_recv[z], even_recv[z])
    return jnp.where(slab == (0 if before else peers - 1), jnp.zeros_like(picked), picked)


def kernel_stack(rounded, target):
    channels = rounded.shape[0]
    width = 3 * channels
    for at in range(9):
        target[at * channels : (at + 1) * channels, :] = rounded[:, at * width : (at + 1) * width]


def own_products(weights, own, kernel, kernel_two, back, stack, product):
    channels = weights.shape[1]
    kernel_stack(weights[0].astype(bf16), kernel)
    products([own[z] for z in range(own.shape[0])], kernel, stack, product)
    kernel_stack(weights[1].astype(bf16), kernel_two)
    turned = weights[1].T
    for at in range(9):
        for e in range(3):
            block = (8 - at) * 3 + 2 - e
            back[at * channels : (at + 1) * channels, e * channels : (e + 1) * channels] = turned[
                block * channels : (block + 1) * channels, :
            ].astype(bf16)


def first_conv(peers, near_even, near_odd, kernel, own_product, first, totals, stack, product):
    slab = lax.axis_index("slab")
    depth, channels, cells = first.shape
    planes = [halo_plane(near_even, near_odd, 0, before, slab, peers) for before in (True, False)]
    products(planes, kernel, stack, product)

    def part(a, b, z):
        if 0 <= z < depth:
            return tap(own_product, a, b, z, channels, cells)
        return tap(product, a, b, 0 if z < 0 else 1, channels, cells)

    s = q = None
    for z in range(depth):
        value = tap_sum(part, z)
        first[z] = value
        s, q = add_to(s, value), add_to(q, value * value)
    send_totals(totals, s, q)


def first_conv_edges(peers, far_even, far_odd, kernel, own_product, near_product, stack, product):
    slab = lax.axis_index("slab")
    cells = stack.shape[1] // 4
    channels = own_product.shape[0] // 9
    depth = own_product.shape[1] // cells
    planes = [
        halo_plane(far_even, far_odd, z, before, slab, peers) for before in (True, False) for z in (0, 1)
    ]
    products(planes, kernel, stack, product, trimmed=True)
    where = {-3: 0, -2: 1, depth + 1: 2, depth + 2: 3}

    def part(a, b, z):
        if 0 <= z < depth:
            return tap(own_product, a, b, z, channels, cells)
        if z in (-1, depth):
            return tap(near_product, a, b, 0 if z < 0 else 1, channels, cells)
        return tap(product, a, b, where[z], channels, cells)

    return [tap_sum(part, z) for z in (-2, -1, depth, depth + 1)]


def second_conv(
    peers, cell_count, rows, first, far_even, far_odd, kernel_one, own_product, near_product, kernel,
    second, totals, stack, product, far_stack, far_product,
):
    edges = first_conv_edges(
        peers, far_even, far_odd, kernel_one, own_product, near_product, far_stack, far_product
    )
    slab = lax.axis_index("slab")
    depth, channels, cells = first.shape
    centre, spread = moments(rows[...], cell_count)

    def plane(z):
        at = z - 2
        source = first[at] if 0 <= at < depth else edges[z if z < 2 else z - depth]
        normed = (source - centre) * spread
        return inside(z, 2, depth, slab, peers, (normed * sigmoid(normed)).astype(bf16))

    products([functools.partial(plane, z) for z in range(depth + 4)], kernel, stack, product, True)
    s = q = None
    for z in range(depth + 2):
        value = depth_sum(product, z, channels, cells)
        second[z] = value
        if 1 <= z < depth + 1:
            s, q = add_to(s, value), add_to(q, value * value)
    send_totals(totals, s, q)


def second_gradient(peers, cell_count, rows, second, cotan, far_even, far_odd, gradient, totals):
    slab = lax.axis_index("slab")
    depth = cotan.shape[0]
    centre, spread = moments(rows[...], cell_count)
    s = q = None
    for z in range(depth + 2):
        if 1 <= z < depth + 1:
            upstream = cotan[z - 1]
        else:
            upstream = halo_plane(far_even, far_odd, FEATURE_HALO - 1, z == 0, slab, peers)
        normed = (second[z] - centre) * spread
        value = upstream.astype(f32) * slope(normed)
        gradient[z] = value
        if 1 <= z < depth + 1:
            s, q = add_to(s, value), add_to(q, value * normed)
    send_totals(totals, s, q)


def back_conv(
    peers, cell_count, rows_one, rows_two, rows, first, second, gradient, kernel,
    cotan_two, gradient_one, normed_one, stack, product,
):
    slab = lax.axis_index("slab")
    extended, channels, cells = second.shape
    depth = extended - 2
    centre, spread = moments(rows_two[...], cell_count)
    mean, crossed = (x / cell_count for x in to_columns(rows[...]))

    def plane(z):
        normed = (second[z] - centre) * spread
        value = (spread * (gradient[z] - mean - normed * crossed)).astype(bf16)
        value = inside(z, 1, depth, slab, peers, value)
        if 1 <= z < depth + 1:
            cotan_two[z - 1] = value
        return value

    products([functools.partial(plane, z) for z in range(extended)], kernel, stack, product, True)
    centre, spread = moments(rows_one[...], cell_count)
    for z in range(depth):
        normed = (first[z] - centre) * spread
        normed_one[z] = normed
        gradient_one[z] = depth_sum(product, z, channels, cells) * slope(normed)


def fill_taps(cotans, taps, at):
    rows, cells = cotans[0].shape
    for z, plane in enumerate(cotans):
        for b in range(3):
            taps[at + b * rows : at + (b + 1) * rows, z * cells : (z + 1) * cells] = row_shift(plane, 1 - b)


def contract(stack, taps, depth, cells):
    windows = [stack[:, a * cells : (a + depth) * cells] for a in range(3)]
    return lax.dot_general(
        jnp.concatenate(windows, axis=0), taps, (((1,), (1,)), ((), ())), preferred_element_type=f32
    )


def extra_rows(length):
    return 8 * pl.cdiv(length + 7, 16)


def parts_of(row, count):
    parts = []
    for _ in range(count):
        part = row.astype(bf16).astype(f32)
        parts.append(part)
        row = row - part
    return parts


def kernel_grads(
    cell_count, rows_one, normed_one, gradient_one, own_stack, near_stack, cotan_two, hidden_stack,
    pieces, stack, taps_one, taps_two, gathered, side, ones_rows,
):
    depth, channels, cells = normed_one.shape
    count, rows, lanes = pieces.shape
    length = gathered.shape[0] // count
    half = rows - length
    _, spread = moments(rows_one[...], cell_count)
    s = q = m = v = None
    for z in range(depth):
        grad, norm = gradient_one[z], normed_one[z]
        s, q = add_to(s, grad), add_to(q, grad * norm)
        m, v = add_to(m, norm), add_to(v, norm * norm)
    s, q, m, v = (jnp.sum(x, axis=1, keepdims=True) for x in (s, q, m, v))
    size = depth * cells
    tilt = (q / size - s / size * (m / size)) / (v / size - m / size * (m / size) + 1.0)
    tilt = tilt.astype(bf16).astype(f32)
    level = (spread * (s / size - tilt * (m / size))).astype(bf16).astype(f32)
    centred, normed = [], []
    for z in range(depth):
        value = spread * (gradient_one[z] - normed_one[z] * tilt) - level
        centred.append(value.astype(bf16))
        normed.append((spread * normed_one[z]).astype(bf16))
    stack[:, :cells] = near_stack[:, :cells]
    stack[:, cells : (depth + 1) * cells] = own_stack[...]
    stack[:, (depth + 1) * cells :] = near_stack[:, cells:]
    width = 3 * channels
    fill_taps(centred, taps_one, 0)
    fill_taps(normed, taps_one, width)
    cell = lax.broadcasted_iota(jnp.int32, (16, cells), 1)
    tap_row = lax.broadcasted_iota(jnp.int32, (16, cells), 0)
    ones = jnp.where(
        ((tap_row == 0) & (cell < cells - W)) | (tap_row == 1) | ((tap_row == 2) & (cell >= W)), 1.0, 0.0
    ).astype(bf16)
    for z in range(depth):
        taps_one[2 * width :, z * cells : (z + 1) * cells] = ones
    fill_taps([cotan_two[z] for z in range(depth)], taps_two, 0)
    grad_one = contract(stack, taps_one[...], depth, cells)
    grad_two = contract(hidden_stack.at[:, cells : (depth + 3) * cells], taps_two[...], depth, cells)
    for b in range(3):
        at = slice(b * 3 * width, (b + 1) * 3 * width)
        span = slice(b * channels, (b + 1) * channels)
        gathered[at, :channels] = grad_one[:, span]
        gathered[at, channels:] = grad_two[:, span]
        side[at, :channels] = grad_one[:, width + b * channels : width + (b + 1) * channels]
    total = 9 * width
    if count * length > total:
        gathered[total:, :] = jnp.zeros((count * length - total, lanes), f32)
        side[total:, :] = jnp.zeros((count * length - total, lanes), f32)
    turned = grad_one[:, 2 * width :].T
    ones_rows[:, :channels] = jnp.zeros((1, channels), f32)
    for b in range(3):
        start = channels + b * 3 * width
        ones_rows[:, start : start + 3 * width] = turned[b : b + 1, :]
    ones_rows[:, channels + total :] = jnp.zeros((1, ones_rows.shape[1] - channels - total), f32)
    totals, fit = to_row(spread * s, q), to_row(level, tilt)
    tail = jnp.concatenate(
        [pltpu.roll(part, channels, 1) for part in parts_of(totals, 3)]
        + parts_of(totals, 2)
        + [pltpu.roll(fit, channels, 1), fit],
        axis=0,
    )
    left = lax.broadcasted_iota(jnp.int32, (half, lanes), 1) < channels
    for j in range(count):
        pieces[j, :length] = gathered[j * length : (j + 1) * length, :].astype(bf16)
        first = side[j * length : j * length + half, :]
        further = jnp.concatenate([tail, ones_rows[:, j * length : j * length + lanes]], axis=0)
        if length > half:
            second = pltpu.roll(side[j * length + half : (j + 1) * length, :], channels, 1)
            further = jnp.concatenate([second, further], axis=0)
        if further.shape[0] < half:
            pad = jnp.zeros((half - further.shape[0], lanes), f32)
            further = jnp.concatenate([further, pad], axis=0)
        pieces[j, length:] = jnp.where(left, first, further).astype(bf16)


def piece_sums(patients, cells, pieces, sums, squares):
    count, rows, lanes = pieces.shape
    length = sums.shape[1]
    half, channels = rows - length, lanes // 2
    peers = count // patients
    start = length + max(length - half, 0)
    further = jnp.concatenate([pieces[c, start : start + 8] for c in range(count)], axis=0)
    starts = (0, 3, 5, 6, 7, 8)
    kinds = len(starts) - 1
    target = lax.broadcasted_iota(jnp.int32, (kinds * count, 8 * count), 0)
    offset = lax.broadcasted_iota(jnp.int32, (kinds * count, 8 * count), 1) - 8 * (target % count)
    picked = offset < 0
    for at in range(kinds):
        picked |= (target // count == at) & (offset >= starts[at]) & (offset < starts[at + 1])
    picked &= offset >= 0
    picks = jnp.dot(jnp.where(picked, 1.0, 0.0).astype(bf16), further, preferred_element_type=f32)
    lower = lax.broadcasted_iota(jnp.int32, (kinds * count, lanes), 1) < channels
    picks = jnp.where(lower, pltpu.roll(picks, channels, 1), 0.0)

    lane = lax.broadcasted_iota(jnp.int32, (1, squares.shape[1]), 1)
    row = jnp.zeros((1, squares.shape[1]), f32)
    for p in range(patients):
        means, crosses, levels, tilts, ones = (
            picks[at * count + p * peers : at * count + (p + 1) * peers] for at in range(kinds)
        )
        means = jnp.sum(means, axis=0, keepdims=True) / (cells * peers) - levels
        crosses = jnp.sum(crosses, axis=0, keepdims=True) / (cells * peers) - tilts
        total = -lax.dot_general(
            ones, means, (((0,), (0,)), ((), ())), precision=lax.Precision.HIGHEST, preferred_element_type=f32
        )[:length]
        for j in range(peers):
            piece = pieces.at[p * peers + j]
            normed = piece[length : length + min(length, half)].astype(f32)
            if length > half:
                second = pltpu.roll(piece[length : 2 * length - half].astype(f32), channels, 1)
                normed = jnp.concatenate([normed, second], axis=0)
            total = total + piece[:length].astype(f32) - crosses[j : j + 1] * normed
        sums[p] = total
        part_of = jnp.sum(jnp.sum(total * total, axis=0, keepdims=True), axis=1, keepdims=True)
        row = jnp.where(lane == p, part_of, row)
    squares[...] = jnp.broadcast_to(row, squares.shape)


def clipped(patients, squares, sums, pieces):
    row = jnp.sum(squares[...], axis=0, keepdims=True)
    factor = clip_bound / jnp.maximum(jnp.sqrt(row), clip_bound)
    total = None
    for p in range(patients):
        total = add_to(total, sums[p] * factor[:, p : p + 1])
    rounded = total.astype(bf16)
    for j in range(pieces.shape[0]):
        pieces[j] = rounded


def update(pieces, weights, prev_state, tree_noise, state_next, weights_next, gathered, state, kernels, sems):
    count, length, lanes = pieces.shape
    width = 3 * (lanes // 2)
    for j in range(count):
        gathered[j * length : (j + 1) * length, :] = pieces[j].astype(f32)

    def block(at):
        row = (at % 3 * 3 + at // 3) * width
        return gathered[row : row + width, :]

    copies = []
    for at in range(0, 9, 2):
        group = range(at, min(at + 2, 9))
        span = slice(at * width, (group[-1] + 1) * width)
        combined = jnp.concatenate([block(i) for i in group], axis=0).T
        state[:, span] = prev_state[:, span] + combined
        kernels[:, span] = weights[:, span] - step_rate * (combined + tree_noise[:, span])
        for source, target in ((state, state_next), (kernels, weights_next)):
            copy = pltpu.make_async_copy(source.at[:, span], target.at[:, span], sems.at[len(copies)])
            copy.start()
            copies.append(copy)
    for copy in copies:
        copy.wait()


def trade(planes, pairs):
    return lax.ppermute(planes, "slab", pairs)


def exchange(rows):
    return lax.all_to_all(rows, "slab", 0, 0)


def per_device(features, cotangent, weights, prev_state, tree_noise):
    peers, patients = lax.axis_size("slab"), lax.axis_size("pat")
    devices = peers * patients
    own = features[0].transpose(1, 0, 2)
    cotan = cotangent[0].transpose(1, 0, 2)
    depth, channels, cells = own.shape
    cell_count = peers * depth * cells
    columns = weights.shape[2]
    rows_shape = sds((peers, 2 * channels), f32)

    def field(planes, dtype):
        return sds((planes, channels, cells), dtype)

    def stack_of(planes):
        return sds((3 * channels, planes * cells), bf16)

    def product_of(planes):
        return sds((9 * channels, planes * cells), f32)

    def scratch_of(shape):
        return pltpu.VMEM(shape.shape, shape.dtype)

    def flops(planes):
        return 2 * 27 * channels * channels * cells * planes

    far = field(FEATURE_HALO - 1 + COTAN_HALO, bf16)
    near_even, near_odd = call(cut_near, (field(1, bf16),) * 2, own, flops=EARLY)
    far_even, far_odd = call(cut_far, (far,) * 2, own, cotan)
    even_pairs = [(i, i ^ 1) for i in range(peers)]
    odd_pairs = [(i, (i + 1) % peers if i % 2 else (i - 1) % peers) for i in range(peers)]
    near_even = trade(near_even, even_pairs)
    near_odd = trade(near_odd, odd_pairs)
    far_even = trade(far_even, even_pairs)
    far_odd = trade(far_odd, odd_pairs)

    kernel_shape = sds((9 * channels, 3 * channels), bf16)
    kernel_one, kernel_two, kernel_back, own_stack, own_product = call(
        own_products,
        (kernel_shape, kernel_shape, kernel_shape, stack_of(depth), product_of(depth)),
        weights, own,
        flops=flops(depth),
    )
    first, totals, near_stack, near_product = call(
        functools.partial(first_conv, peers),
        (field(depth, f32), rows_shape, stack_of(2), product_of(2)),
        near_even, near_odd, kernel_one, own_product,
        flops=flops(2),
    )
    rows_one = exchange(totals)
    second, totals, hidden_stack = call(
        functools.partial(second_conv, peers, cell_count),
        (field(depth + 2, f32), rows_shape, stack_of(depth + 4)),
        rows_one, first, far_even, far_odd, kernel_one, own_product, near_product, kernel_two,
        scratch=[scratch_of(product_of(depth + 4)), scratch_of(stack_of(4)), scratch_of(product_of(4))],
        flops=flops(depth + 4),
    )
    rows_two = exchange(totals)
    gradient_two, totals = call(
        functools.partial(second_gradient, peers, cell_count),
        (field(depth + 2, f32), rows_shape),
        rows_two, second, cotan, far_even, far_odd,
    )
    rows_three = exchange(totals)
    cotan_two, gradient_one, normed_one = call(
        functools.partial(back_conv, peers, cell_count),
        (field(depth, bf16), field(depth, f32), field(depth, f32)),
        rows_one, rows_two, rows_three, first, second, gradient_two, kernel_back,
        scratch=[scratch_of(stack_of(depth + 2)), scratch_of(product_of(depth + 2))],
        flops=flops(depth + 2),
    )

    length = 8 * pl.cdiv(columns, 8 * devices)
    taps = pltpu.VMEM((3 * channels, depth * cells), bf16)
    pieces = call(
        functools.partial(kernel_grads, cell_count),
        sds((devices, length + extra_rows(length), 2 * channels), bf16),
        rows_one, normed_one, gradient_one, own_stack, near_stack, cotan_two, hidden_stack,
        scratch=[
            scratch_of(stack_of(depth + 2)),
            pltpu.VMEM((6 * channels + 16, depth * cells), bf16),
            taps,
            pltpu.VMEM((devices * length, 2 * channels), f32),
            pltpu.VMEM((devices * length, 2 * channels), f32),
            pltpu.VMEM((1, devices * length + 4 * channels), f32),
        ],
        flops=3 * flops(depth),
    )
    pieces = lax.all_to_all(pieces, AXES, 0, 0)
    sums, squares = call(
        functools.partial(piece_sums, patients, depth * cells),
        (sds((patients, length, 2 * channels), f32), sds((devices, 128), f32)),
        pieces,
    )
    pieces_shape = sds((peers, length, 2 * channels), bf16)
    squares = lax.all_to_all(squares, AXES, 0, 0)
    pieces = call(functools.partial(clipped, patients), pieces_shape, squares, sums)
    pieces = lax.all_gather(lax.all_to_all(pieces, "slab", 0, 0), "pat", tiled=True)
    flat = (2 * channels, columns)
    vmem, hbm = pl.BlockSpec(memory_space=pltpu.VMEM), pl.BlockSpec(memory_space=pl.ANY)
    state_next, weights_next = pl.pallas_call(
        update,
        out_shape=(sds(flat, f32), sds(flat, f32)),
        in_specs=[vmem] * 4,
        out_specs=(hbm, hbm),
        scratch_shapes=[
            pltpu.VMEM((devices * length, 2 * channels), f32),
            pltpu.VMEM(flat, f32),
            pltpu.VMEM(flat, f32),
            pltpu.SemaphoreType.DMA((10,)),
        ],
        compiler_params=pltpu.CompilerParams(vmem_limit_bytes=18 * 2**20),
    )(pieces, weights.reshape(flat), prev_state.reshape(flat), tree_noise.reshape(flat))
    return (state_next.reshape(weights.shape), weights_next.reshape(weights.shape))


def solution(mesh):
    return jax.shard_map(
        per_device,
        mesh=mesh,
        in_specs=(P("pat", None, "slab", None), P("pat", None, "slab", None), P(), P(), P()),
        out_specs=(P(), P()),
        check_vma=False,
    )
```
